128 devices in a mesh: exp: 32 (over y, x, core), imp: 4 (over z).
Axes of the slice: x: 4, y: 4, z: 4, core: 2. Of those that a mesh axis runs over, the one named last changes fastest.
Arguments:
- flows: bfloat16 [512, 256, 256], P(('exp', 'imp')), may hold values from 0 to 8, as said below
- routing: int32 [128, 4, 1], P(('exp', 'imp')), may hold values from -1 to 3, as said below
- tile_block: int32 [512], P(('exp', 'imp')), may hold values from 0 to 7, as said below
- exp_country: int32 [16384], P('exp'), may hold values from 0 to 127, never falling along the last dimension, each value on 1 to 256 neighbouring positions
- imp_country: int32 [4096], P('imp'), may hold values from 0 to 127, never falling along the last dimension, each value on 1 to 64 neighbouring positions
Outputs:
- exporter_effects: float32 [16384], P('exp')
- importer_effects: float32 [4096], P('imp')
- pair_effects: float32 [128, 128], replicated
The draws below stay inside these ranges and needn't reach their ends.
Inputs may be any that keep to these rules, and one draw needn't show every extreme that they name: `routing`: entry [d, t, s] names a slot of device d routed to imp index t, or is -1. Each slot is named at most once. The devices of one exp index route at most 3 named slots to each imp index in all, and exactly 3 to some imp index of every exp index; each entry names at most one slot, and some entry of some device does name one; in every exp index some device names all 4 of its slots. `tile_block`: r * 4 + c for the slot's local exporter block r and local importer block c; distinct within a device. `exp_country`: never falls along the exporter-years; every country has 1 to 256 of them. `imp_country`: never falls along the importer-years; every country has 1 to 64 of them. Positive flows.
All inputs are finite; a program needn't handle non-finite values.
Results may differ from the reference program's by a relative error of at most 0.0003.
Values may be sent and summed in bfloat16 or wider, within the bound.
A program may use at most 64 MiB of HBM per device.

```python
import math
import jax
import jax.numpy as jnp
import numpy as np

BS = 256
RB_DEV = 2
TS = 4
NCE = 128
NCI = 128
NEWTON = 2
CG = 2
CB_DEV = 4
TR = 3
SB = 1
TILES = 512
NA = 16384
NB = 4096
N_EXP = 32
N_IMP = 4


def route_group(group_key):
    key_extra, key_heavy, key_pick, key_slots, key_turn = jax.random.split(group_key, 5)
    extra_total = jax.random.randint(key_extra, (), 0, N_IMP)
    group_total = N_IMP * (TR - 1) + 1 + extra_total
    heavy_member = jax.random.randint(key_heavy, (), 0, N_IMP)
    spare_units = group_total - TS - (N_IMP - 1)
    places = (N_IMP - 1) * (TS - 1)
    shuffle = jax.random.permutation(key_pick, places)
    chosen = (shuffle < spare_units).astype(jnp.int32).reshape(N_IMP - 1, TS - 1)
    others = 1 + jnp.sum(chosen, axis=1)
    member = jnp.arange(N_IMP, dtype=jnp.int32)
    other_index = jnp.clip(member - (member > heavy_member).astype(jnp.int32), 0, N_IMP - 2)
    counts = jnp.where(member == heavy_member, TS, others[other_index])
    starts = jnp.cumsum(counts) - counts
    slot_keys = jax.random.split(key_slots, N_IMP)
    slot_order = jax.vmap(lambda sub_key: jax.random.permutation(sub_key, TS))(slot_keys).astype(jnp.int32)
    start_turn = jax.random.randint(key_turn, (), 0, N_IMP)
    within = jnp.arange(TS, dtype=jnp.int32)
    target = (starts[:, None] + within[None, :] + start_turn) % N_IMP
    slot_place = jnp.broadcast_to((within // N_IMP)[None, :], (N_IMP, TS))
    slot_value = jnp.where(within[None, :] < counts[:, None], slot_order, -1).astype(jnp.int32)
    sender = jnp.broadcast_to(member[:, None], (N_IMP, TS))
    send_table = jnp.full((N_IMP, N_IMP, SB), -1, jnp.int32)
    return send_table.at[sender, target, slot_place].set(slot_value)


def draw_routing(key, part):
    group_keys = jax.random.split(jax.random.fold_in(key, 11), N_EXP)
    return jax.vmap(route_group)(group_keys).reshape(N_EXP * N_IMP, N_IMP, SB)


def draw_tile_block(key, part):
    device_keys = jax.random.split(jax.random.fold_in(key, 23), N_EXP * N_IMP)
    picked = jax.vmap(lambda sub_key: jax.random.permutation(sub_key, RB_DEV * CB_DEV)[:TS])(device_keys)
    return picked.reshape(-1).astype(jnp.int32)


def draw_flows(key, part):
    key_rows, key_cols, key_cells = jax.random.split(jax.random.fold_in(key, 37), 3)
    col_scale = jnp.exp(jax.random.uniform(key_cols, (TILES, 1, BS), jnp.float32, math.log(0.5), math.log(2.0)))
    row_scale = jnp.exp(jax.random.uniform(key_rows, (TILES, BS, 1), jnp.float32, math.log(0.5), math.log(2.0)))
    cell_part = jax.random.uniform(key_cells, (TILES, BS, BS), jnp.float32, 0.5, 1.5)
    return (row_scale * col_scale * cell_part).astype(jnp.bfloat16)


def split_up(count, total, bound, slope):
    weights = [(1 << 20) // math.isqrt(rank ** slope) + 1 for rank in range(2, count + 1)]
    spare, given = total - bound - (count - 1), [1] * (count - 1)
    while spare > 0:
        candidates = [i for i in range(count - 1) if given[i] < bound]
        mass, budget = sum([weights[i] for i in candidates]), spare
        for i in candidates:
            more = min(bound - given[i], max(1, budget * weights[i] // mass), spare)
            given[i] = given[i] + more
            spare = spare - more
    return np.array([bound] + given)


def uneven_parts(rng, number_of, total, bound, slope):
    if number_of == 2:
        one = jax.random.randint(rng, (), max(1, total - bound), min(bound, total - 1) + 1)
        return jnp.stack([one, total - one])
    tallies = jnp.asarray(split_up(number_of, total, bound, slope), jnp.int32)
    couples = (number_of - 1) // 2
    source_of, taker = tallies[1:1 + 2 * couples:2], tallies[2:2 + 2 * couples:2]
    slack = jnp.minimum(source_of - 1, bound - taker)
    moved = jax.random.randint(jax.random.fold_in(rng, 1), (couples,), 0, 1 << 20) % (slack + 1)
    tallies = tallies.at[1:1 + 2 * couples:2].set(source_of - moved).at[2:2 + 2 * couples:2].set(taker + moved)
    return tallies[jax.random.permutation(jax.random.fold_in(rng, 2), number_of)]


def setup_inputs(seed: int = 0) -> dict:
    arg_keys = jax.random.split(jax.random.key(seed), 6)
    flows = draw_flows(jax.random.fold_in(arg_keys[5], 71), 0)
    routing = draw_routing(jax.random.fold_in(arg_keys[5], 71), 0)
    tile_block = draw_tile_block(jax.random.fold_in(arg_keys[5], 71), 0)
    exp_country = jnp.searchsorted(jnp.cumsum(uneven_parts(arg_keys[3], NCE, NA, 2 * NA // NCE, 1)), jnp.arange(NA), side="right").astype(jnp.int32)
    imp_country = jnp.searchsorted(jnp.cumsum(uneven_parts(arg_keys[4], NCI, NB, 2 * NB // NCI, 1)), jnp.arange(NB), side="right").astype(jnp.int32)
    return dict(flows=flows, routing=routing, tile_block=tile_block, exp_country=exp_country, imp_country=imp_country)


ridge_weight = 64.0


def combine(anchor, factor, change):
    return tuple(current + factor * addend for current, addend in zip(anchor, change))


def inner_product(left_vec, right_vec):
    return jnp.sum(left_vec[0] * right_vec[0]) + jnp.sum(left_vec[1] * right_vec[1]) + jnp.sum(left_vec[2] * right_vec[2])


def reference(flows, routing, tile_block, exp_country, imp_country):
    tile_index = jnp.arange(TILES, dtype=jnp.int32)
    device = tile_index // TS
    slot_number = tile_index % TS
    is_live = jnp.any(routing[device] == slot_number[:, None, None], axis=(1, 2))
    row_block = (device // N_IMP) * RB_DEV + tile_block // CB_DEV
    col_block = (device % N_IMP) * CB_DEV + tile_block % CB_DEV
    within = jnp.arange(BS, dtype=jnp.int32)
    row_ids = (row_block[:, None] * BS + within[None, :]).astype(jnp.int32)
    col_ids = (col_block[:, None] * BS + within[None, :]).astype(jnp.int32)
    pair_ids = (exp_country[row_ids][:, :, None] * NCI + imp_country[col_ids][:, None, :]).astype(jnp.int32)
    live_mask = is_live[:, None, None]
    observed = flows.astype(jnp.float32)

    def expand(effects):
        return effects[0][row_ids][:, :, None] + effects[1][col_ids][:, None, :] + effects[2].reshape(-1)[pair_ids]

    def collect(weighted):
        part_rows = jax.ops.segment_sum(jnp.sum(weighted, axis=2).reshape(-1), row_ids.reshape(-1), num_segments=NA)
        part_cols = jax.ops.segment_sum(jnp.sum(weighted, axis=1).reshape(-1), col_ids.reshape(-1), num_segments=NB)
        part_pairs = jax.ops.segment_sum(weighted.reshape(-1), pair_ids.reshape(-1), num_segments=NCE * NCI)
        return (part_rows, part_cols, part_pairs.reshape(NCE, NCI))

    effects = (jnp.zeros((NA,), jnp.float32), jnp.zeros((NB,), jnp.float32), jnp.zeros((NCE, NCI), jnp.float32))
    for newton in range(NEWTON):
        mean_rate = jnp.where(live_mask, jnp.exp(expand(effects)), 0.0)
        gradient = collect(jnp.where(live_mask, observed - mean_rate, 0.0))
        residual = combine(gradient, -ridge_weight, effects)
        update = tuple(jnp.zeros_like(current) for current in effects)
        direction = residual
        norm_now = inner_product(residual, residual)
        for cg_sweep in range(CG):
            image_vec = combine(collect(mean_rate * expand(direction)), ridge_weight, direction)
            step_size = norm_now / inner_product(direction, image_vec)
            update = combine(update, step_size, direction)
            residual = combine(residual, -step_size, image_vec)
            norm_next = inner_product(residual, residual)
            direction = combine(residual, norm_next / norm_now, direction)
            norm_now = norm_next
        effects = combine(effects, 1.0, update)
    return (effects[0], effects[1], effects[2])
```

```python
import functools

import jax
import jax.numpy as jnp
from jax import lax
from jax.experimental import pallas as pl
from jax.experimental.pallas import tpu as pltpu
from jax.sharding import PartitionSpec as P

MESH = pl.DeviceIdType.MESH
RIDGE = 64.0
NC = 128
SIDE = 256
SLOTS = 4
F32 = jnp.float32
BF16 = jnp.bfloat16


def split(x):
    hi = x.astype(BF16)
    lo = (x - hi.astype(F32)).astype(BF16)
    return hi, lo


def dot(x, y):
    return lax.dot_general(x, y, (((1,), (0,)), ((), ())), preferred_element_type=F32)


def dot_nt(x, y):
    return lax.dot_general(x, y, (((1,), (1,)), ((), ())), preferred_element_type=F32)


def kernel(
    dims,
    routing,
    tile_block,
    flows,
    exp_ids,
    imp_ids,
    a_out,
    b_out,
    g_out,
    fbuf,
    row_t,
    row_s,
    col_t,
    col_s,
    x0,
    xq,
    mu,
    ubuf,
    vbuf,
    va,
    vb,
    r0g,
    qg,
    eg,
    own,
    gown,
    zb,
    bb,
    yb,
    hs,
    hb,
    sb,
    pb,
    rsb,
    rxb,
    gfull,
    fsem,
    zs,
    zr,
    bs,
    br,
    ys,
    yr,
    hss,
    hr,
    ss,
    sr,
    ps,
    pr,
    rss,
    rsr,
    rxs,
    rxr,
    ags,
    agr,
):
    Y, XC, Z = dims
    E, YZ = Y * XC, Y * Z
    rows_chunk = NC // YZ
    e = lax.axis_index("exp")
    m = lax.axis_index("imp")
    y = lax.div(e, XC)
    j = lax.rem(e, XC)
    p = y * Z + m

    xc_dev = [(y * XC + lax.rem(j + k, XC), m) for k in range(1, XC)]
    z_dev = [(e, lax.rem(m + k, Z)) for k in range(1, Z)]
    y_dev = [(lax.rem(y + k, Y) * XC + j, m) for k in range(1, Y)]
    yz_idx = [(lax.rem(y + ky, Y), lax.rem(m + kz, Z)) for ky in range(Y) for kz in range(Z)][1:]
    yz_dev = [(yy * XC + j, mm) for yy, mm in yz_idx]
    h_dev = [(lax.rem(e + 1, E), m), (lax.rem(e + E - 1, E), m)]

    barrier = pltpu.get_barrier_semaphore()
    greet = xc_dev + yz_dev + h_dev
    for dev in greet:
        pl.semaphore_signal(barrier, inc=1, device_id=dev, device_id_type=MESH)

    fcopy = pltpu.make_async_copy(flows, fbuf, fsem)
    fcopy.start()

    pending = []

    def push(src, dst, send_sem, recv_sem, dev):
        copy = pltpu.make_async_remote_copy(
            src_ref=src, dst_ref=dst, send_sem=send_sem, recv_sem=recv_sem, device_id=dev, device_id_type=MESH
        )
        copy.start()
        pending.append(copy)
        return copy

    def arrive(copies):
        for copy in copies:
            copy.wait_recv()

    riota = lax.broadcasted_iota(jnp.int32, (NC, NC), 0)
    ciota = lax.broadcasted_iota(jnp.int32, (NC, NC), 1)
    riota_f, ciota_f = riota.astype(F32), ciota.astype(F32)
    row_blk, col_blk, live = [], [], []
    for k in range(SLOTS):
        blk = tile_block[k]
        row_blk.append(lax.div(blk, 4))
        col_blk.append(lax.rem(blk, 4))
        hit = jnp.int32(0)
        for t in range(routing.shape[0]):
            hit = hit | jnp.where(routing[t] == k, 1, 0)
        live.append(hit)
    erow = [exp_ids[pl.ds(2 * row_blk[k] + h, 1), :] for k in range(SLOTS) for h in range(2)]
    irow = [imp_ids[pl.ds(2 * col_blk[k] + h, 1), :] for k in range(SLOTS) for h in range(2)]
    ids_t = jnp.concatenate(
        [v.astype(F32) for v in erow + irow] + [jnp.zeros((NC - 4 * SLOTS, NC), F32)], axis=0
    ).T
    for q in range(2 * SLOTS):
        k, h = divmod(q, 2)
        row_t[:, NC * q : NC * (q + 1)] = jnp.where(riota == erow[q], 1.0, 0.0).astype(BF16)
        row_s[NC * q : NC * (q + 1), :] = jnp.where(ciota_f == ids_t[:, q : q + 1], 1.0, 0.0).astype(BF16)
        hot = jnp.where(riota == irow[q], 1.0, 0.0).astype(BF16)
        col_t[k, 0:NC, NC * h : NC * (h + 1)] = hot
        col_t[k, NC : 2 * NC, NC * h : NC * (h + 1)] = hot
        col_s[NC * q : NC * (q + 1), :] = jnp.where(
            ciota_f == ids_t[:, 2 * SLOTS + q : 2 * SLOTS + q + 1], 1.0, 0.0
        ).astype(BF16)
    eids, iids = exp_ids[...].astype(F32), imp_ids[...].astype(F32)

    def least(v):
        return jnp.min(jnp.min(v, axis=0, keepdims=True), axis=1, keepdims=True)

    rf = jnp.broadcast_to(least(eids), (1, NC))
    rl = jnp.broadcast_to(-least(-eids), (1, NC))
    cf = jnp.broadcast_to(least(iids), (1, NC))
    cl = jnp.broadcast_to(-least(-iids), (1, NC))
    lane = lax.broadcasted_iota(jnp.int32, (1, NC), 1).astype(F32)
    zero_row = jnp.zeros((1, NC), F32)
    ends = jnp.concatenate(
        [jnp.where(lane == cf, 1.0, 0.0), jnp.where(lane == cl, 1.0, 0.0)] + [zero_row] * 6, axis=0
    ).astype(BF16)
    ones8 = jnp.ones((8, 2 * NC), BF16)
    row_w = [[jnp.where(row_blk[k] == c, 1.0, 0.0) for c in range(2)] for k in range(SLOTS)]
    col_w = [[jnp.where(col_blk[k] == c, 1.0, 0.0) for c in range(4)] for k in range(SLOTS)]

    def keep(k, x):
        return jnp.where(jnp.full(x.shape, live[k]) > 0, x, 0.0)

    def collect(cells):
        sums = []
        for k in range(SLOTS):
            w = cells(k)
            hi, lo = split(w)
            cs = col_s[SIDE * k : SIDE * (k + 1), :]
            vhi, vlo = split(dot(hi, cs) + dot(lo, cs))
            vbuf[SIDE * k : SIDE * (k + 1), 0:NC] = vhi
            vbuf[SIDE * k : SIDE * (k + 1), NC : 2 * NC] = vlo
            sums.append(jnp.sum(w, axis=0, keepdims=True))
        v = vbuf[...]
        wide = dot(row_t[...], v)
        table = wide[:, 0:NC] + wide[:, NC : 2 * NC]
        rsum = dot_nt(ones8, v)
        arows, brows = [], []
        for c in range(2):
            for h in range(2):
                arows.append(
                    sum(
                        row_w[k][c] * rsum[0:1, SIDE * k + NC * h : SIDE * k + NC * (h + 1)]
                        for k in range(SLOTS)
                    )
                )
        for c in range(4):
            for h in range(2):
                brows.append(sum(col_w[k][c] * sums[k][:, NC * h : NC * (h + 1)] for k in range(SLOTS)))
        return table, arows, brows

    def vec_send(r, table, arows, brows, scal):
        hi, lo = split(table)
        edge = dot_nt(ends, jnp.concatenate([hi, lo], axis=0))
        edge = edge[:, 0:NC] + edge[:, NC : 2 * NC]
        first = jnp.sum(jnp.where(riota_f == rf, table, 0.0), axis=0, keepdims=True)
        last = jnp.sum(jnp.where(riota_f == rl, table, 0.0), axis=0, keepdims=True)
        width = 8 if scal is None else 16
        bb[r, j, 0:8, :] = jnp.concatenate(brows, axis=0)
        if scal is not None:
            bb[r, j, 8:16, :] = scal
        src = bb.at[r, j, pl.ds(0, width)]
        bcopies = [push(src, src, bs.at[r, k], br.at[r, k], dev) for k, dev in enumerate(xc_dev)]
        zb[r, m, 0:8, :] = jnp.concatenate(arows + [edge[0:1], edge[1:2], first, last], axis=0)
        width = 8
        if r == 0:
            zb[r, m, 8:16, :] = jnp.concatenate([cf, cl] + [zero_row] * 6, axis=0)
            width = 16
        src = zb.at[r, m, pl.ds(0, width)]
        zcopies = [push(src, src, zs.at[r, k], zr.at[r, k], dev) for k, dev in enumerate(z_dev)]
        return zcopies, bcopies

    def vec_turn(r, zcopies, bcopies, scal):
        arrive(bcopies)
        yb[r, y] = sum(bb[r, k, 0:8, :] for k in range(XC))
        src = yb.at[r, y]
        ycopies = [push(src, src, ys.at[r, k], yr.at[r, k], dev) for k, dev in enumerate(y_dev)]
        pcopies = []
        if scal is not None:
            pcopies = scal_turn(scal, sum(bb[r, k, 8:16, :] for k in range(XC)))
        arrive(zcopies)
        edge = sum(zb[r, k, 0:8, :] for k in range(Z))
        hs[r] = jnp.concatenate([edge[6:7], edge[7:8], rf, rl] + [zero_row] * 4, axis=0)
        hcopies = [
            push(hs.at[r], hb.at[r, 0], hss.at[r, 0], hr.at[r, 0], h_dev[0]),
            push(hs.at[r], hb.at[r, 1], hss.at[r, 1], hr.at[r, 1], h_dev[1]),
        ]
        return edge[0:4], ycopies, hcopies, pcopies

    def scal_turn(s, total):
        pb[s, p] = total
        src = pb.at[s, p]
        return [push(src, src, ps.at[s, k], pr.at[s, k], dev) for k, dev in enumerate(yz_dev)]

    def scal_total(s, pcopies):
        arrive(pcopies)
        total = sum(pb[s, k] for k in range(YZ))
        return jnp.sum(total, axis=1, keepdims=True)

    def columns(r, avec):
        va[0:4, :] = avec
        tiles = [va[pl.ds(2 * row_blk[k] + h, 1), :] for k in range(SLOTS) for h in range(2)]
        prev = zb[r, lax.rem(m + Z - 1, Z), 5:6, :]
        after = zb[r, lax.rem(m + 1, Z), 4:5, :]
        return jnp.concatenate(tiles + [prev, after, jnp.zeros((NC - 10, NC), F32)], axis=0).T

    def vec_end(r, table, cols, ycopies, hcopies):
        cl_prev = zb[0, lax.rem(m + Z - 1, Z), 9:10, :]
        cf_next = zb[0, lax.rem(m + 1, Z), 8:9, :]
        table = table + jnp.where(ciota_f == cl_prev, cols[:, 8:9], 0.0)
        table = table + jnp.where(ciota_f == cf_next, cols[:, 9:10], 0.0)
        arrive(hcopies)
        rl_prev, rf_next = hb[0, 0, 3:4, :], hb[0, 1, 2:3, :]
        table = table + jnp.where(riota_f == rl_prev, hb[r, 0, 1:2, :], 0.0)
        table = table + jnp.where(riota_f == rf_next, hb[r, 1, 0:1, :], 0.0)
        arrive(ycopies)
        bvec = sum(yb[r, k] for k in range(Y))
        if r == 0:
            skip_r = jnp.where(rl_prev == rf, 1.0, 0.0)
            skip_c = jnp.where(cl_prev == cf, 1.0, 0.0)
            mine = (riota_f >= rf + skip_r) & (riota_f <= rl) & (ciota_f >= cf + skip_c) & (ciota_f <= cl)
            own[...] = jnp.where(mine, 1.0, 0.0)
        return table, bvec

    def expand(gval, cols, bvec):
        hi, lo = split(gval)
        ubuf[...] = dot(row_s[...], jnp.concatenate([hi, lo], axis=1)).astype(BF16)
        vb[...] = bvec

        def tile(k):
            brow = jnp.concatenate([vb[pl.ds(2 * col_blk[k] + h, 1), :] for h in range(2)], axis=1)
            acol = jnp.concatenate([cols[:, 2 * k + h : 2 * k + h + 1] for h in range(2)], axis=0)
            return dot(ubuf[SIDE * k : SIDE * (k + 1), :], col_t[k]) + acol + brow

        return tile

    def fold(x):
        x = jnp.sum(x.reshape(SIDE // 8, 8, SIDE), axis=0)
        return x[:, 0:NC] + x[:, NC:SIDE]

    def lanes(x):
        return jnp.sum(x, axis=0, keepdims=True)

    def inner(u, v):
        total = lanes(u[0] * v[0]) * (1.0 / Z) + lanes(u[1] * v[1]) * (1.0 / E)
        return total + lanes(own[...] * u[2] * v[2])

    effects = None
    for newton in range(2):
        r = 2 * newton
        if newton == 0:

            def cells(k):
                mu[k] = keep(k, jnp.ones((SIDE, SIDE), F32))
                return keep(k, fbuf[k].astype(F32) - 1.0)

            fcopy.wait()
        else:

            def cells(k):
                rate = keep(k, jnp.exp(c0 * x0[k] + c1 * (x0[k] - step * xq[k])))
                mu[k] = rate
                return keep(k, fbuf[k].astype(F32)) - rate

        table, arows, brows = collect(cells)
        if newton == 0:
            pl.semaphore_wait(barrier, len(greet))
        zc, bc = vec_send(r, table, arows, brows, None)
        ra, yc, hc, _ = vec_turn(r, zc, bc, None)
        if newton:
            ra = ra - RIDGE * effects[0]
        cols = columns(r, ra)
        rg, rb = vec_end(r, table, cols, yc, hc)
        if newton:
            rg = rg - RIDGE * eg[...]
            rb = rb - RIDGE * effects[1]
        r0g[...] = rg
        res = (ra, rb, rg)
        tile = expand(rg, cols, rb)
        quad = []

        def cells(k):
            x = tile(k)
            x0[k] = x
            w = mu[k] * x
            quad.append(fold(w * x))
            return w

        table, arows, brows = collect(cells)
        scal = jnp.concatenate([inner(res, res), lanes(sum(quad))] + [zero_row] * 6, axis=0)
        zc, bc = vec_send(r + 1, table, arows, brows, scal)
        qa, yc, hc, pc = vec_turn(r + 1, zc, bc, r)
        qa = qa + RIDGE * ra
        cols = columns(r + 1, qa)
        qgv, qb = vec_end(r + 1, table, cols, yc, hc)
        qgv = qgv + RIDGE * r0g[...]
        qb = qb + RIDGE * rb
        qg[...] = qgv
        tile = expand(qgv, cols, qb)
        for k in range(SLOTS):
            xq[k] = tile(k)
        total = scal_total(r, pc)
        rr = total[0:1]
        rhr = total[1:2] + RIDGE * rr
        step = rr / rhr
        quad = []
        for k in range(SLOTS):
            x = x0[k] - step * xq[k]
            quad.append(fold(mu[k] * x * x))
        qvec = (qa, qb, qg[...])
        res1 = (ra - step * qa, rb - step * qb, r0g[...] - step * qg[...])
        sb[newton, j] = jnp.concatenate(
            [inner(res1, res1), lanes(sum(quad)), inner(res1, qvec)] + [zero_row] * 5, axis=0
        )
        src = sb.at[newton, j]
        sc = [push(src, src, ss.at[newton, k], sr.at[newton, k], dev) for k, dev in enumerate(xc_dev)]
        arrive(sc)
        pc = scal_turn(r + 1, sum(sb[newton, k] for k in range(XC)))
        total = scal_total(r + 1, pc)
        rr1 = total[0:1]
        beta = rr1 / rr
        curve = total[1:2] + RIDGE * rr1 + 2.0 * beta * total[2:3] + beta * beta * rhr
        c1 = rr1 / curve
        c0 = step + c1 * beta
        moved = [
            c0 * u + c1 * v
            for u, v in zip((ra, rb, r0g[...]), (ra - step * qa, rb - step * qb, r0g[...] - step * qg[...]))
        ]
        if newton == 0:
            effects = (moved[0], moved[1])
            eg[...] = moved[2]
        else:
            a_out[...] = effects[0] + moved[0]
            b_out[...] = effects[1] + moved[1]
            gown[...] = (eg[...] + moved[2]) * own[...]

    rsb[p] = gown[pl.ds(p * rows_chunk, rows_chunk), :]
    copies = [
        push(
            gown.at[pl.ds((yy * Z + mm) * rows_chunk, rows_chunk)],
            rsb.at[p],
            rss.at[k],
            rsr.at[k],
            yz_dev[k],
        )
        for k, (yy, mm) in enumerate(yz_idx)
    ]
    arrive(copies)
    rxb[j] = sum(rsb[k] for k in range(YZ))
    copies = [push(rxb.at[j], rxb.at[j], rxs.at[k], rxr.at[k], dev) for k, dev in enumerate(xc_dev)]
    arrive(copies)
    mine = gfull.at[pl.ds(p * rows_chunk, rows_chunk)]
    gfull[pl.ds(p * rows_chunk, rows_chunk), :] = sum(rxb[k] for k in range(XC))
    copies = [push(mine, mine, ags.at[k], agr.at[k], dev) for k, dev in enumerate(yz_dev)]
    arrive(copies)
    g_out[...] = gfull[...]
    for copy in pending:
        copy.wait_send()


def per_device(dims, flows, routing, tile_block, exp_country, imp_country):
    Y, XC, Z = dims
    YZ = Y * Z
    dma = pltpu.SemaphoreType.DMA
    vmem = functools.partial(pl.BlockSpec, memory_space=pltpu.VMEM)
    smem = functools.partial(pl.BlockSpec, memory_space=pltpu.SMEM)
    cells = SLOTS * SIDE
    pair = (NC, NC)
    sems = []
    for count in ((4, Z - 1), (4, XC - 1), (4, Y - 1), (4, 2), (2, XC - 1), (4, YZ - 1), (YZ - 1,), (XC - 1,), (YZ - 1,)):
        sems += [dma(count), dma(count)]
    a, b, g = pl.pallas_call(
        functools.partial(kernel, dims),
        out_shape=(
            jax.ShapeDtypeStruct((4, NC), F32),
            jax.ShapeDtypeStruct((8, NC), F32),
            jax.ShapeDtypeStruct(pair, F32),
        ),
        in_specs=[smem(), smem(), pl.BlockSpec(memory_space=pl.ANY), vmem(), vmem()],
        out_specs=(vmem(), vmem(), vmem()),
        scratch_shapes=[
            pltpu.VMEM((SLOTS, SIDE, SIDE), BF16),
            pltpu.VMEM((NC, cells), BF16),
            pltpu.VMEM((cells, NC), BF16),
            pltpu.VMEM((SLOTS, 2 * NC, SIDE), BF16),
            pltpu.VMEM((cells, NC), BF16),
            pltpu.VMEM((SLOTS, SIDE, SIDE), F32),
            pltpu.VMEM((SLOTS, SIDE, SIDE), F32),
            pltpu.VMEM((SLOTS, SIDE, SIDE), F32),
            pltpu.VMEM((cells, 2 * NC), BF16),
            pltpu.VMEM((cells, 2 * NC), BF16),
            pltpu.VMEM((8, NC), F32),
            pltpu.VMEM((8, NC), F32),
            pltpu.VMEM(pair, F32),
            pltpu.VMEM(pair, F32),
            pltpu.VMEM(pair, F32),
            pltpu.VMEM(pair, F32),
            pltpu.VMEM(pair, F32),
            pltpu.VMEM((4, Z, 16, NC), F32),
            pltpu.VMEM((4, XC, 16, NC), F32),
            pltpu.VMEM((4, Y, 8, NC), F32),
            pltpu.VMEM((4, 8, NC), F32),
            pltpu.VMEM((4, 2, 8, NC), F32),
            pltpu.VMEM((2, XC, 8, NC), F32),
            pltpu.VMEM((4, YZ, 8, NC), F32),
            pltpu.VMEM((YZ, NC // YZ, NC), F32),
            pltpu.VMEM((XC, NC // YZ, NC), F32),
            pltpu.VMEM(pair, F32),
            dma,
        ]
        + sems,
        compiler_params=pltpu.CompilerParams(collective_id=0, has_side_effects=True),
        name="gravity",
    )(
        routing.reshape(-1),
        tile_block,
        flows,
        exp_country.reshape(4, NC),
        imp_country.reshape(8, NC),
    )
    return a.reshape(-1), b.reshape(-1), g


def solution(mesh, side=8):
    dims = (mesh.shape["exp"] // side, side, mesh.shape["imp"])
    placed = (
        P(("exp", "imp"), None, None),
        P(("exp", "imp"), None, None),
        P(("exp", "imp")),
        P("exp"),
        P("imp"),
    )
    return jax.shard_map(
        functools.partial(per_device, dims),
        mesh=mesh,
        in_specs=placed,
        out_specs=(P("exp"), P("imp"), P()),
        check_vma=False,
    )
```

```python
import functools

import jax
import jax.numpy as jnp
from jax import lax
from jax.experimental import pallas as pl
from jax.experimental.pallas import tpu as pltpu
from jax.sharding import PartitionSpec as P

MESH = pl.DeviceIdType.MESH
RIDGE = 64.0
NC = 128
SIDE = 256
SLOTS = 4
F32 = jnp.float32
BF16 = jnp.bfloat16


def split(x):
    hi = x.astype(BF16)
    lo = (x - hi.astype(F32)).astype(BF16)
    return hi, lo


def dot(x, y):
    return lax.dot_general(x, y, (((1,), (0,)), ((), ())), preferred_element_type=F32)


def dot_nt(x, y):
    return lax.dot_general(x, y, (((1,), (1,)), ((), ())), preferred_element_type=F32)


def order(offsets):
    far = lambda off: sum(min(o, 4 - o) for o in off)
    return sorted((off for off in offsets if any(off)), key=far, reverse=True)


def kernel(
    dims,
    routing,
    tile_block,
    flows,
    exp_ids,
    imp_ids,
    a_out,
    b_out,
    g_out,
    fbuf,
    row_t,
    row_s,
    col_t,
    col_s,
    x0,
    xq,
    mu,
    ubuf,
    vbuf,
    va,
    vb,
    r0g,
    qg,
    eg,
    own,
    tabs,
    zb,
    cb,
    yb,
    hs,
    hb,
    cs,
    ps,
    rsb,
    rxb,
    agb,
    fsem,
    z_s,
    z_r,
    c_s,
    c_r,
    y_s,
    y_r,
    h_s,
    h_r,
    cs_s,
    cs_r,
    ps_s,
    ps_r,
    rs_s,
    rs_r,
    rx_s,
    rx_r,
    ag_s,
    ag_r,
):
    Y, XN, Z = dims
    E, XY = 2 * Y * XN, Y * XN
    chunk = NC // XY
    e = lax.axis_index("exp")
    m = lax.axis_index("imp")
    chip = lax.div(e, 2)
    core = lax.rem(e, 2)
    y = lax.div(chip, XN)
    x = lax.rem(chip, XN)
    zc = m * 2 + core

    def device(yy, xx, cc, mm):
        return ((yy * XN + xx) * 2 + cc, mm)

    def step_to(at, off, size):
        return lax.rem(at + off, size) if off else at

    c_dev = [device(y, x, 1 - core, m)]
    z_dev = [(e, lax.rem(m + k, Z)) for k in range(1, Z)]
    xy_at = [
        (step_to(y, oy, Y), step_to(x, ox, XN)) for oy, ox in order([(i, k) for i in range(Y) for k in range(XN)])
    ]
    xy_dev = [device(yy, xx, core, m) for yy, xx in xy_at]
    xyz_dev = [
        device(step_to(y, oy, Y), step_to(x, ox, XN), core, step_to(m, oz, Z))
        for oy, ox, oz in order([(i, k, q) for i in range(Y) for k in range(XN) for q in range(Z)])
    ]
    zc_dev = [
        device(y, x, 1 - core if oc else core, step_to(m, oz, Z))
        for oz, oc in order([(i, k) for i in range(Z) for k in range(2)])
    ]
    after, before = lax.rem(e + 1, E), lax.rem(e + E - 1, E)
    h_dev = [(after, lax.rem(m + k, Z)) for k in range(Z)], [(before, lax.rem(m + k, Z)) for k in range(Z)]
    xy = y * XN + x

    barrier = pltpu.get_barrier_semaphore()
    greet = xy_dev + h_dev[0] + h_dev[1] + zc_dev
    for dev in greet:
        pl.semaphore_signal(barrier, inc=1, device_id=dev, device_id_type=MESH)

    fcopy = pltpu.make_async_copy(flows, fbuf, fsem)
    fcopy.start()

    pending = []

    def push(src, dst, send_sem, recv_sem, dev):
        copy = pltpu.make_async_remote_copy(
            src_ref=src, dst_ref=dst, send_sem=send_sem, recv_sem=recv_sem, device_id=dev, device_id_type=MESH
        )
        copy.start()
        pending.append(copy)
        return copy

    def fan(src, dst, send_sem, recv_sem, devs):
        return [push(src, dst, send_sem.at[k], recv_sem.at[k], dev) for k, dev in enumerate(devs)]

    def arrive(copies):
        for copy in copies:
            copy.wait_recv()

    riota = lax.broadcasted_iota(jnp.int32, (NC, NC), 0)
    ciota = lax.broadcasted_iota(jnp.int32, (NC, NC), 1)
    riota_f, ciota_f = riota.astype(F32), ciota.astype(F32)
    row_blk, col_blk, live = [], [], []
    for k in range(SLOTS):
        blk = tile_block[k]
        row_blk.append(lax.div(blk, 4))
        col_blk.append(lax.rem(blk, 4))
        hit = jnp.int32(0)
        for t in range(routing.shape[0]):
            hit = hit | jnp.where(routing[t] == k, 1, 0)
        live.append(hit)
    erow = [exp_ids[pl.ds(2 * row_blk[k] + h, 1), :] for k in range(SLOTS) for h in range(2)]
    irow = [imp_ids[pl.ds(2 * col_blk[k] + h, 1), :] for k in range(SLOTS) for h in range(2)]
    ids_t = jnp.concatenate(
        [v.astype(F32) for v in erow + irow] + [jnp.zeros((NC - 4 * SLOTS, NC), F32)], axis=0
    ).T
    for q in range(2 * SLOTS):
        k, h = divmod(q, 2)
        row_t[:, NC * q : NC * (q + 1)] = jnp.where(riota == erow[q], 1.0, 0.0).astype(BF16)
        row_s[NC * q : NC * (q + 1), :] = jnp.where(ciota_f == ids_t[:, q : q + 1], 1.0, 0.0).astype(BF16)
        hot = jnp.where(riota == irow[q], 1.0, 0.0).astype(BF16)
        col_t[k, 0:NC, NC * h : NC * (h + 1)] = hot
        col_t[k, NC : 2 * NC, NC * h : NC * (h + 1)] = hot
        col_s[NC * q : NC * (q + 1), :] = jnp.where(
            ciota_f == ids_t[:, 2 * SLOTS + q : 2 * SLOTS + q + 1], 1.0, 0.0
        ).astype(BF16)
    eids, iids = exp_ids[...].astype(F32), imp_ids[...].astype(F32)

    def least(v):
        return jnp.min(jnp.min(v, axis=0, keepdims=True), axis=1, keepdims=True)

    rf = jnp.broadcast_to(least(eids), (1, NC))
    rl = jnp.broadcast_to(-least(-eids), (1, NC))
    cf = jnp.broadcast_to(least(iids), (1, NC))
    cl = jnp.broadcast_to(-least(-iids), (1, NC))
    lane = lax.broadcasted_iota(jnp.int32, (1, NC), 1).astype(F32)
    zero_row = jnp.zeros((1, NC), F32)
    ends = jnp.concatenate(
        [jnp.where(lane == cf, 1.0, 0.0), jnp.where(lane == cl, 1.0, 0.0)] + [zero_row] * 6, axis=0
    ).astype(BF16)
    ones8 = jnp.ones((8, 2 * NC), BF16)
    row_w = [[jnp.where(row_blk[k] == c, 1.0, 0.0) for c in range(2)] for k in range(SLOTS)]
    col_w = [[jnp.where(col_blk[k] == c, 1.0, 0.0) for c in range(4)] for k in range(SLOTS)]

    def keep(k, v):
        return jnp.where(jnp.full(v.shape, live[k]) > 0, v, 0.0)

    def collect(cells):
        sums = []
        for k in range(SLOTS):
            w = cells(k)
            hi, lo = split(w)
            hot = col_s[SIDE * k : SIDE * (k + 1), :]
            vhi, vlo = split(dot(hi, hot) + dot(lo, hot))
            vbuf[SIDE * k : SIDE * (k + 1), 0:NC] = vhi
            vbuf[SIDE * k : SIDE * (k + 1), NC : 2 * NC] = vlo
            sums.append(jnp.sum(w, axis=0, keepdims=True))
        brows = []
        for c in range(4):
            for h in range(2):
                brows.append(sum(col_w[k][c] * sums[k][:, NC * h : NC * (h + 1)] for k in range(SLOTS)))
        return jnp.concatenate(brows, axis=0)

    def b_send(r, bpart):
        cb[r, core] = bpart
        return fan(cb.at[r, core], cb.at[r, core], c_s.at[r], c_r.at[r], c_dev)

    def table_sums():
        v = vbuf[...]
        wide = dot(row_t[...], v)
        table = wide[:, 0:NC] + wide[:, NC : 2 * NC]
        rsum = dot_nt(ones8, v)
        arows = []
        for c in range(2):
            for h in range(2):
                arows.append(
                    sum(
                        row_w[k][c] * rsum[0:1, SIDE * k + NC * h : SIDE * k + NC * (h + 1)]
                        for k in range(SLOTS)
                    )
                )
        return table, arows

    def table_send(r, table, arows):
        first = jnp.sum(jnp.where(riota_f == rf, table, 0.0), axis=0, keepdims=True)
        last = jnp.sum(jnp.where(riota_f == rl, table, 0.0), axis=0, keepdims=True)
        hs[r, 0] = jnp.concatenate([last, rl], axis=0)
        hs[r, 1] = jnp.concatenate([first, rf], axis=0)
        hcopies = []
        for side in range(2):
            hcopies += fan(hs.at[r, side], hb.at[r, side, m], h_s.at[r, side], h_r.at[r, side], h_dev[side])
        hi, lo = split(table)
        edge = dot_nt(ends, jnp.concatenate([hi, lo], axis=0))
        edge = edge[:, 0:NC] + edge[:, NC : 2 * NC]
        zb[r, m] = jnp.concatenate(arows + [edge[0:1], edge[1:2], cf, cl], axis=0)
        zcopies = fan(zb.at[r, m], zb.at[r, m], z_s.at[r], z_r.at[r], z_dev)
        return zcopies, hcopies

    def b_turn(r, ccopies):
        arrive(ccopies)
        yb[r, xy] = cb[r, 0] + cb[r, 1]
        return fan(yb.at[r, xy], yb.at[r, xy], y_s.at[r], y_r.at[r], xy_dev)

    def scal_send(s, rows):
        rows = jnp.sum(jnp.concatenate(rows + [zero_row] * (8 - len(rows)), axis=0), axis=1, keepdims=True)
        cs[s, core] = sum(jnp.where(lane == float(k), rows[k : k + 1], 0.0) for k in range(3))
        return fan(cs.at[s, core], cs.at[s, core], cs_s.at[s], cs_r.at[s], c_dev)

    def scal_turn(s, copies):
        arrive(copies)
        place = xy * Z + m
        ps[s, place] = cs[s, 0] + cs[s, 1]
        return fan(ps.at[s, place], ps.at[s, place], ps_s.at[s], ps_r.at[s], xyz_dev)

    def scal_total(s, copies):
        arrive(copies)
        total = sum(ps[s, k] for k in range(XY * Z))
        return [total[:, k : k + 1] for k in range(3)]

    def columns(r, avec):
        va[0:4, :] = avec
        tiles = [va[pl.ds(2 * row_blk[k] + h, 1), :] for k in range(SLOTS) for h in range(2)]
        prev = zb[r, lax.rem(m + Z - 1, Z), 5:6, :]
        nxt = zb[r, lax.rem(m + 1, Z), 4:5, :]
        return jnp.concatenate(tiles + [prev, nxt, jnp.zeros((NC - 10, NC), F32)], axis=0).T

    def table_end(r, table, cols, hcopies):
        cl_prev = zb[r, lax.rem(m + Z - 1, Z), 7:8, :]
        cf_next = zb[r, lax.rem(m + 1, Z), 6:7, :]
        table = table + jnp.where(ciota_f == cl_prev, cols[:, 8:9], 0.0)
        table = table + jnp.where(ciota_f == cf_next, cols[:, 9:10], 0.0)
        arrive(hcopies)
        from_prev, from_next = (sum(hb[r, side, k] for k in range(Z)) for side in range(2))
        rl_prev, rf_next = hb[r, 0, 0, 1:2, :], hb[r, 1, 0, 1:2, :]
        table = table + jnp.where(riota_f == rl_prev, from_prev[0:1], 0.0)
        table = table + jnp.where(riota_f == rf_next, from_next[0:1], 0.0)
        if r == 0:
            skip_r = jnp.where(rl_prev == rf, 1.0, 0.0)
            skip_c = jnp.where(cl_prev == cf, 1.0, 0.0)
            mine = (riota_f >= rf + skip_r) & (riota_f <= rl) & (ciota_f >= cf + skip_c) & (ciota_f <= cl)
            own[...] = jnp.where(mine, 1.0, 0.0)
        return table

    def b_end(r, ycopies):
        arrive(ycopies)
        return sum(yb[r, k] for k in range(XY))

    def expand(gval, cols, bvec):
        hi, lo = split(gval)
        ubuf[...] = dot(row_s[...], jnp.concatenate([hi, lo], axis=1)).astype(BF16)
        vb[...] = bvec

        def tile(k):
            brow = jnp.concatenate([vb[pl.ds(2 * col_blk[k] + h, 1), :] for h in range(2)], axis=1)
            acol = jnp.concatenate([cols[:, 2 * k + h : 2 * k + h + 1] for h in range(2)], axis=0)
            return dot(ubuf[SIDE * k : SIDE * (k + 1), :], col_t[k]) + acol + brow

        return tile

    def fold(v):
        v = jnp.sum(v.reshape(SIDE // 8, 8, SIDE), axis=0)
        return v[:, 0:NC] + v[:, NC:SIDE]

    def lanes(v):
        return jnp.sum(v, axis=0, keepdims=True)

    def inner(u, v):
        total = lanes(u[0] * v[0]) * (1.0 / Z) + lanes(u[1] * v[1]) * (1.0 / E)
        return total + lanes(own[...] * u[2] * v[2])

    def scatter(lo, hi, part):
        src = tabs.at[pl.ds(lo, hi - lo)]
        rsb[xy, lo:hi] = tabs[lo:hi, pl.ds(xy * chunk, chunk), :]
        return [
            push(
                src.at[:, pl.ds((yy * XN + xx) * chunk, chunk)],
                rsb.at[xy, pl.ds(lo, hi - lo)],
                rs_s.at[part, k],
                rs_r.at[part, k],
                xy_dev[k],
            )
            for k, (yy, xx) in enumerate(xy_at)
        ]

    effects = None
    for newton in range(2):
        final = newton == 1
        r = 2 * newton
        if not final:

            def cells(k):
                mu[k] = keep(k, jnp.ones((SIDE, SIDE), F32))
                return keep(k, fbuf[k].astype(F32) - 1.0)

            fcopy.wait()
        else:

            def cells(k):
                rate = keep(k, jnp.exp(c0 * x0[k] + c1 * (x0[k] - step * xq[k])))
                mu[k] = rate
                return keep(k, fbuf[k].astype(F32)) - rate

        bpart = collect(cells)
        if not final:
            pl.semaphore_wait(barrier, len(greet))
        cc = b_send(r, bpart)
        table, arows = table_sums()
        zcp, hcp = table_send(r, table, arows)
        yc = b_turn(r, cc)
        arrive(zcp)
        ra = sum(zb[r, k, 0:4, :] for k in range(Z))
        if final:
            ra = ra - RIDGE * effects[0]
        cols = columns(r, ra)
        rg = table_end(r, table, cols, hcp)
        if final:
            rg = rg - RIDGE * eg[...]
        rb = b_end(r, yc)
        if final:
            rb = rb - RIDGE * effects[1]
        r0g[...] = rg
        if final:
            tabs[0] = eg[...] * own[...]
            tabs[1] = rg * own[...]
            rs_copies = scatter(0, 2, 0)
        res = (ra, rb, rg)
        tile = expand(rg, cols, rb)
        quad = []

        def cells(k):
            v = tile(k)
            x0[k] = v
            w = mu[k] * v
            quad.append(fold(w * v))
            return w

        bpart = collect(cells)
        sc = scal_send(r, [inner(res, res), lanes(sum(quad))])
        cc = b_send(r + 1, bpart)
        table, arows = table_sums()
        pc = scal_turn(r, sc)
        zcp, hcp = table_send(r + 1, table, arows)
        yc = b_turn(r + 1, cc)
        if final:
            tabs[2] = table
            rs_copies += scatter(2, 3, 1)
        arrive(zcp)
        qa = sum(zb[r + 1, k, 0:4, :] for k in range(Z)) + RIDGE * ra
        cols = columns(r + 1, qa)
        qgv = table_end(r + 1, table, cols, hcp) + RIDGE * r0g[...]
        qg[...] = qgv
        if final:
            arrive(rs_copies)
            rxb[zc] = sum(rsb[k] for k in range(XY))
            rx_copies = fan(rxb.at[zc], rxb.at[zc], rx_s, rx_r, zc_dev)
        qb = b_end(r + 1, yc) + RIDGE * rb
        tile = expand(qgv, cols, qb)
        for k in range(SLOTS):
            xq[k] = tile(k)
        rr, rhr, _ = scal_total(r, pc)
        rhr = rhr + RIDGE * rr
        step = rr / rhr

        quad = []
        for k in range(SLOTS):
            v = x0[k] - step * xq[k]
            quad.append(fold(mu[k] * v * v))
        qvec = (qa, qb, qg[...])
        res1 = (ra - step * qa, rb - step * qb, r0g[...] - step * qg[...])
        sc = scal_send(r + 1, [inner(res1, res1), lanes(sum(quad)), inner(res1, qvec)])
        pc = scal_turn(r + 1, sc)
        if final:
            arrive(rx_copies)
            agb[xy] = sum(rxb[k] for k in range(2 * Z))
            ag_copies = fan(agb.at[xy], agb.at[xy], ag_s, ag_r, xy_dev)
        rr1, curve, cross = scal_total(r + 1, pc)
        beta = rr1 / rr
        curve = curve + RIDGE * rr1 + 2.0 * beta * cross + beta * beta * rhr
        c1 = rr1 / curve
        c0 = step + c1 * beta
        da = c0 * ra + c1 * (ra - step * qa)
        db = c0 * rb + c1 * (rb - step * qb)
        if not final:
            effects = (da, db)
            eg[...] = c0 * r0g[...] + c1 * (r0g[...] - step * qg[...])
        else:
            a_out[...] = effects[0] + da
            b_out[...] = effects[1] + db
            arrive(ag_copies)
            for k in range(XY):
                was, res0, img = agb[k, 0], agb[k, 1], agb[k, 2]
                img = img + RIDGE * res0
                g_out[chunk * k : chunk * (k + 1), :] = was + (c0 * res0 + c1 * (res0 - step * img))
    for copy in pending:
        copy.wait_send()


def per_device(dims, flows, routing, tile_block, exp_country, imp_country):
    Y, XN, Z = dims
    XY = Y * XN
    chunk = NC // XY
    dma = pltpu.SemaphoreType.DMA
    vmem = functools.partial(pl.BlockSpec, memory_space=pltpu.VMEM)
    smem = functools.partial(pl.BlockSpec, memory_space=pltpu.SMEM)
    cells = SLOTS * SIDE
    pair = (NC, NC)
    sems = []
    for count in (
        (4, Z - 1),
        (4, 1),
        (4, XY - 1),
        (4, 2, Z),
        (4, 1),
        (4, XY * Z - 1),
        (2, XY - 1),
        (2 * Z - 1,),
        (XY - 1,),
    ):
        sems += [dma(count), dma(count)]
    a, b, g = pl.pallas_call(
        functools.partial(kernel, dims),
        out_shape=(
            jax.ShapeDtypeStruct((4, NC), F32),
            jax.ShapeDtypeStruct((8, NC), F32),
            jax.ShapeDtypeStruct(pair, F32),
        ),
        in_specs=[smem(), smem(), pl.BlockSpec(memory_space=pl.ANY), vmem(), vmem()],
        out_specs=(vmem(), vmem(), vmem()),
        scratch_shapes=[
            pltpu.VMEM((SLOTS, SIDE, SIDE), BF16),
            pltpu.VMEM((NC, cells), BF16),
            pltpu.VMEM((cells, NC), BF16),
            pltpu.VMEM((SLOTS, 2 * NC, SIDE), BF16),
            pltpu.VMEM((cells, NC), BF16),
            pltpu.VMEM((SLOTS, SIDE, SIDE), F32),
            pltpu.VMEM((SLOTS, SIDE, SIDE), F32),
            pltpu.VMEM((SLOTS, SIDE, SIDE), F32),
            pltpu.VMEM((cells, 2 * NC), BF16),
            pltpu.VMEM((cells, 2 * NC), BF16),
            pltpu.VMEM((8, NC), F32),
            pltpu.VMEM((8, NC), F32),
            pltpu.VMEM(pair, F32),
            pltpu.VMEM(pair, F32),
            pltpu.VMEM(pair, F32),
            pltpu.VMEM(pair, F32),
            pltpu.VMEM((3,) + pair, F32),
            pltpu.VMEM((4, Z, 8, NC), F32),
            pltpu.VMEM((4, 2, 8, NC), F32),
            pltpu.VMEM((4, XY, 8, NC), F32),
            pltpu.VMEM((4, 2, 2, NC), F32),
            pltpu.VMEM((4, 2, Z, 2, NC), F32),
            pltpu.VMEM((4, 2, 1, NC), F32),
            pltpu.VMEM((4, XY * Z, 1, NC), F32),
            pltpu.VMEM((XY, 3, chunk, NC), F32),
            pltpu.VMEM((2 * Z, 3, chunk, NC), F32),
            pltpu.VMEM((XY, 3, chunk, NC), F32),
            dma,
        ]
        + sems,
        compiler_params=pltpu.CompilerParams(collective_id=0, has_side_effects=True),
        name="gravity",
    )(
        routing.reshape(-1),
        tile_block,
        flows,
        exp_country.reshape(4, NC),
        imp_country.reshape(8, NC),
    )
    return a.reshape(-1), b.reshape(-1), g


def solution(mesh, xn=4):
    dims = (mesh.shape["exp"] // (2 * xn), xn, mesh.shape["imp"])
    placed = (
        P(("exp", "imp"), None, None),
        P(("exp", "imp"), None, None),
        P(("exp", "imp")),
        P("exp"),
        P("imp"),
    )
    return jax.shard_map(
        functools.partial(per_device, dims),
        mesh=mesh,
        in_specs=placed,
        out_specs=(P("exp"), P("imp"), P()),
        check_vma=False,
    )
```

```python
import functools

import jax
import jax.numpy as jnp
from jax import lax
from jax.experimental import pallas as pl
from jax.experimental.pallas import tpu as pltpu
from jax.sharding import PartitionSpec as P

MESH = pl.DeviceIdType.MESH
RIDGE = 64.0
NC = 128
SIDE = 256
SLOTS = 4
F32 = jnp.float32
BF16 = jnp.bfloat16


def split(x):
    hi = x.astype(BF16)
    lo = (x - hi.astype(F32)).astype(BF16)
    return hi, lo


def dot(x, y):
    return lax.dot_general(x, y, (((1,), (0,)), ((), ())), preferred_element_type=F32)


def dot_nt(x, y):
    return lax.dot_general(x, y, (((1,), (1,)), ((), ())), preferred_element_type=F32)


def order(offsets):
    far = lambda off: sum(min(o, 4 - o) for o in off)
    return sorted((off for off in offsets if any(off)), key=far, reverse=True)


def kernel(
    dims,
    routing,
    tile_block,
    flows,
    exp_ids,
    imp_ids,
    a_out,
    b_out,
    g_out,
    fbuf,
    row_t,
    row_s,
    col_t,
    col_s,
    x0,
    xq,
    mu,
    ubuf,
    vbuf,
    va,
    vb,
    r0g,
    qg,
    eg,
    own,
    tabs,
    zb,
    bb,
    hs,
    hb,
    ps,
    rsb,
    rxb,
    agb,
    fsem,
    z_sem,
    b_sem,
    h_sem,
    p_sem,
    rs_sem,
    rx_sem,
    ag_sem,
):
    Y, XN, Z = dims
    E, XY = 2 * Y * XN, Y * XN
    chunk = NC // XY
    e = lax.axis_index("exp")
    m = lax.axis_index("imp")
    chip = lax.div(e, 2)
    core = lax.rem(e, 2)
    y = lax.div(chip, XN)
    x = lax.rem(chip, XN)
    zc = m * 2 + core

    def device(yy, xx, cc, mm):
        return ((yy * XN + xx) * 2 + cc, mm)

    def step_to(at, off, size):
        return lax.rem(at + off, size) if off else at

    z_dev = [(e, lax.rem(m + k, Z)) for k in range(1, Z)]
    xy_at = [
        (step_to(y, oy, Y), step_to(x, ox, XN)) for oy, ox in order([(i, k) for i in range(Y) for k in range(XN)])
    ]
    xy_dev = [device(yy, xx, core, m) for yy, xx in xy_at]

    def shift(oy, ox, oz, oc):
        return device(step_to(y, oy, Y), step_to(x, ox, XN), 1 - core if oc else core, step_to(m, oz, Z))

    ranges = [(i, k, q, c) for i in range(Y) for k in range(XN) for q in range(Z) for c in range(2)]
    all_dev = [shift(*off) for off in order(ranges)]
    plane_dev = [shift(*off) for off in order([off for off in ranges if off[2] == 0])]
    zc_dev = [
        device(y, x, 1 - core if oc else core, step_to(m, oz, Z))
        for oz, oc in order([(i, k) for i in range(Z) for k in range(2)])
    ]
    after, before = lax.rem(e + 1, E), lax.rem(e + E - 1, E)
    h_dev = [(after, lax.rem(m + k, Z)) for k in range(Z)], [(before, lax.rem(m + k, Z)) for k in range(Z)]
    xy = y * XN + x

    barrier = pltpu.get_barrier_semaphore()
    greet = plane_dev + h_dev[0] + h_dev[1] + zc_dev
    for dev in greet:
        pl.semaphore_signal(barrier, inc=1, device_id=dev, device_id_type=MESH)

    fcopy = pltpu.make_async_copy(flows, fbuf, fsem)
    fcopy.start()

    def push(src, dst, sems, dev):
        pltpu.make_async_remote_copy(
            src_ref=src, dst_ref=dst, send_sem=sems.at[0], recv_sem=sems.at[1], device_id=dev, device_id_type=MESH
        ).start()

    def fan(src, sems, devs):
        for dev in devs:
            push(src, src, sems, dev)

    def arrive(whole, sems):
        for k in (1, 0):
            pltpu.make_async_copy(whole, whole, sems.at[k]).wait()

    riota = lax.broadcasted_iota(jnp.int32, (NC, NC), 0)
    ciota = lax.broadcasted_iota(jnp.int32, (NC, NC), 1)
    riota_f, ciota_f = riota.astype(F32), ciota.astype(F32)
    row_blk, col_blk, live = [], [], []
    for k in range(SLOTS):
        blk = tile_block[k]
        row_blk.append(lax.div(blk, 4))
        col_blk.append(lax.rem(blk, 4))
        hit = jnp.int32(0)
        for t in range(routing.shape[0]):
            hit = hit | jnp.where(routing[t] == k, 1, 0)
        live.append(hit)
    erow = [exp_ids[pl.ds(2 * row_blk[k] + h, 1), :] for k in range(SLOTS) for h in range(2)]
    irow = [imp_ids[pl.ds(2 * col_blk[k] + h, 1), :] for k in range(SLOTS) for h in range(2)]
    ids_t = jnp.concatenate(
        [v.astype(F32) for v in erow + irow] + [jnp.zeros((NC - 4 * SLOTS, NC), F32)], axis=0
    ).T
    for q in range(2 * SLOTS):
        k, h = divmod(q, 2)
        row_t[:, NC * q : NC * (q + 1)] = jnp.where(riota == erow[q], 1.0, 0.0).astype(BF16)
        row_s[NC * q : NC * (q + 1), :] = jnp.where(ciota_f == ids_t[:, q : q + 1], 1.0, 0.0).astype(BF16)
        hot = jnp.where(riota == irow[q], 1.0, 0.0).astype(BF16)
        col_t[k, 0:NC, NC * h : NC * (h + 1)] = hot
        col_t[k, NC : 2 * NC, NC * h : NC * (h + 1)] = hot
        col_s[NC * q : NC * (q + 1), :] = jnp.where(
            ciota_f == ids_t[:, 2 * SLOTS + q : 2 * SLOTS + q + 1], 1.0, 0.0
        ).astype(BF16)
    eids, iids = exp_ids[...].astype(F32), imp_ids[...].astype(F32)

    def least(v):
        return jnp.min(jnp.min(v, axis=0, keepdims=True), axis=1, keepdims=True)

    rf = jnp.broadcast_to(least(eids), (1, NC))
    rl = jnp.broadcast_to(-least(-eids), (1, NC))
    cf = jnp.broadcast_to(least(iids), (1, NC))
    cl = jnp.broadcast_to(-least(-iids), (1, NC))
    lane = lax.broadcasted_iota(jnp.int32, (1, NC), 1).astype(F32)
    zero_row = jnp.zeros((1, NC), F32)
    ends = jnp.concatenate(
        [jnp.where(lane == cf, 1.0, 0.0), jnp.where(lane == cl, 1.0, 0.0)] + [zero_row] * 6, axis=0
    ).astype(BF16)
    ones8 = jnp.ones((8, 2 * NC), BF16)
    row_w = [[jnp.where(row_blk[k] == c, 1.0, 0.0) for c in range(2)] for k in range(SLOTS)]
    col_w = [[jnp.where(col_blk[k] == c, 1.0, 0.0) for c in range(4)] for k in range(SLOTS)]

    def keep(k, v):
        return jnp.where(jnp.full(v.shape, live[k]) > 0, v, 0.0)

    def collect(cells):
        sums = []
        for k in range(SLOTS):
            w = cells(k)
            hi, lo = split(w)
            hot = col_s[SIDE * k : SIDE * (k + 1), :]
            vhi, vlo = split(dot(hi, hot) + dot(lo, hot))
            vbuf[SIDE * k : SIDE * (k + 1), 0:NC] = vhi
            vbuf[SIDE * k : SIDE * (k + 1), NC : 2 * NC] = vlo
            sums.append(jnp.sum(w, axis=0, keepdims=True))
        brows = []
        for c in range(4):
            for h in range(2):
                brows.append(sum(col_w[k][c] * sums[k][:, NC * h : NC * (h + 1)] for k in range(SLOTS)))
        return jnp.concatenate(brows, axis=0)

    def b_send(r, bpart):
        bb[r, e] = bpart
        fan(bb.at[r, e], b_sem.at[r], plane_dev)

    def table_sums():
        v = vbuf[...]
        wide = dot(row_t[...], v)
        table = wide[:, 0:NC] + wide[:, NC : 2 * NC]
        rsum = dot_nt(ones8, v)
        arows = []
        for c in range(2):
            for h in range(2):
                arows.append(
                    sum(
                        row_w[k][c] * rsum[0:1, SIDE * k + NC * h : SIDE * k + NC * (h + 1)]
                        for k in range(SLOTS)
                    )
                )
        return table, arows

    def table_send(r, table, arows):
        first = jnp.sum(jnp.where(riota_f == rf, table, 0.0), axis=0, keepdims=True)
        last = jnp.sum(jnp.where(riota_f == rl, table, 0.0), axis=0, keepdims=True)
        hs[r, 0] = jnp.concatenate([last, rl], axis=0)
        hs[r, 1] = jnp.concatenate([first, rf], axis=0)
        for side in range(2):
            for dev in h_dev[side]:
                push(hs.at[r, side], hb.at[r, side, m], h_sem.at[r], dev)
        hi, lo = split(table)
        edge = dot_nt(ends, jnp.concatenate([hi, lo], axis=0))
        edge = edge[:, 0:NC] + edge[:, NC : 2 * NC]
        zb[r, m] = jnp.concatenate(arows + [edge[0:1], edge[1:2], cf, cl], axis=0)
        fan(zb.at[r, m], z_sem.at[r], z_dev)

    def scal_send(s, rows):
        rows = jnp.sum(jnp.concatenate(rows + [zero_row] * (8 - len(rows)), axis=0), axis=1, keepdims=True)
        place = e * Z + m
        ps[s, pl.ds(place, 1), :] = sum(jnp.where(lane == float(k), rows[k : k + 1], 0.0) for k in range(3))
        fan(ps.at[s, pl.ds(place, 1)], p_sem.at[s], all_dev)

    def scal_total(s):
        arrive(ps.at[s, pl.ds(0, E * Z - 1)], p_sem.at[s])
        total = jnp.sum(ps[s], axis=0, keepdims=True)
        return [total[:, k : k + 1] for k in range(3)]

    def columns(r, avec):
        va[0:4, :] = avec
        tiles = [va[pl.ds(2 * row_blk[k] + h, 1), :] for k in range(SLOTS) for h in range(2)]
        prev = zb[r, lax.rem(m + Z - 1, Z), 5:6, :]
        nxt = zb[r, lax.rem(m + 1, Z), 4:5, :]
        return jnp.concatenate(tiles + [prev, nxt, jnp.zeros((NC - 10, NC), F32)], axis=0).T

    def table_end(r, table, cols):
        cl_prev = zb[r, lax.rem(m + Z - 1, Z), 7:8, :]
        cf_next = zb[r, lax.rem(m + 1, Z), 6:7, :]
        table = table + jnp.where(ciota_f == cl_prev, cols[:, 8:9], 0.0)
        table = table + jnp.where(ciota_f == cf_next, cols[:, 9:10], 0.0)
        arrive(hb.at[r], h_sem.at[r])
        from_prev, from_next = (sum(hb[r, side, k] for k in range(Z)) for side in range(2))
        rl_prev, rf_next = hb[r, 0, 0, 1:2, :], hb[r, 1, 0, 1:2, :]
        table = table + jnp.where(riota_f == rl_prev, from_prev[0:1], 0.0)
        table = table + jnp.where(riota_f == rf_next, from_next[0:1], 0.0)
        if r == 0:
            skip_r = jnp.where(rl_prev == rf, 1.0, 0.0)
            skip_c = jnp.where(cl_prev == cf, 1.0, 0.0)
            mine = (riota_f >= rf + skip_r) & (riota_f <= rl) & (ciota_f >= cf + skip_c) & (ciota_f <= cl)
            own[...] = jnp.where(mine, 1.0, 0.0)
        return table

    def z_end(r):
        arrive(zb.at[r, pl.ds(0, Z - 1)], z_sem.at[r])
        return sum(zb[r, k, 0:4, :] for k in range(Z))

    def b_end(r):
        arrive(bb.at[r, pl.ds(0, E - 1)], b_sem.at[r])
        return sum(bb[r, k] for k in range(E))

    def expand(gval, cols, bvec):
        hi, lo = split(gval)
        ubuf[...] = dot(row_s[...], jnp.concatenate([hi, lo], axis=1)).astype(BF16)
        vb[...] = bvec

        def tile(k):
            brow = jnp.concatenate([vb[pl.ds(2 * col_blk[k] + h, 1), :] for h in range(2)], axis=1)
            acol = jnp.concatenate([cols[:, 2 * k + h : 2 * k + h + 1] for h in range(2)], axis=0)
            return dot(ubuf[SIDE * k : SIDE * (k + 1), :], col_t[k]) + acol + brow

        return tile

    def fold(v):
        v = jnp.sum(v.reshape(SIDE // 8, 8, SIDE), axis=0)
        return v[:, 0:NC] + v[:, NC:SIDE]

    def lanes(v):
        return jnp.sum(v, axis=0, keepdims=True)

    def inner(u, v):
        total = lanes(u[0] * v[0]) * (1.0 / Z) + lanes(u[1] * v[1]) * (1.0 / E)
        return total + lanes(own[...] * u[2] * v[2])

    def scatter(lo, hi):
        src = tabs.at[pl.ds(lo, hi - lo)]
        rsb[xy, lo:hi] = tabs[lo:hi, pl.ds(xy * chunk, chunk), :]
        for (yy, xx), dev in zip(xy_at, xy_dev):
            push(src.at[:, pl.ds((yy * XN + xx) * chunk, chunk)], rsb.at[xy, pl.ds(lo, hi - lo)], rs_sem, dev)

    effects = None
    for newton in range(2):
        final = newton == 1
        r = 2 * newton
        if not final:

            def cells(k):
                mu[k] = keep(k, jnp.ones((SIDE, SIDE), F32))
                return keep(k, fbuf[k].astype(F32) - 1.0)

            fcopy.wait()
        else:

            def cells(k):
                rate = keep(k, jnp.exp(c0 * x0[k] + c1 * (x0[k] - step * xq[k])))
                mu[k] = rate
                return keep(k, fbuf[k].astype(F32)) - rate

        bpart = collect(cells)
        if not final:
            pl.semaphore_wait(barrier, len(greet))
        b_send(r, bpart)
        table, arows = table_sums()
        table_send(r, table, arows)
        ra = z_end(r)
        if final:
            ra = ra - RIDGE * effects[0]
        cols = columns(r, ra)
        rg = table_end(r, table, cols)
        if final:
            rg = rg - RIDGE * eg[...]
        rb = b_end(r)
        if final:
            rb = rb - RIDGE * effects[1]
        r0g[...] = rg
        if final:
            tabs[0] = eg[...] * own[...]
            tabs[1] = rg * own[...]
            scatter(0, 2)
        res = (ra, rb, rg)
        tile = expand(rg, cols, rb)
        quad = []

        def cells(k):
            v = tile(k)
            x0[k] = v
            w = mu[k] * v
            quad.append(fold(w * v))
            return w

        bpart = collect(cells)
        scal_send(r, [inner(res, res), lanes(sum(quad))])
        b_send(r + 1, bpart)
        table, arows = table_sums()
        table_send(r + 1, table, arows)
        if final:
            tabs[2] = table
            scatter(2, 3)
        qa = z_end(r + 1) + RIDGE * ra
        cols = columns(r + 1, qa)
        qgv = table_end(r + 1, table, cols) + RIDGE * r0g[...]
        qg[...] = qgv
        if final:
            arrive(rsb.at[pl.ds(0, XY - 1)], rs_sem)
            rxb[zc] = sum(rsb[k] for k in range(XY))
            fan(rxb.at[zc], rx_sem, zc_dev)
        qb = b_end(r + 1) + RIDGE * rb
        tile = expand(qgv, cols, qb)
        for k in range(SLOTS):
            xq[k] = tile(k)
        rr, rhr, _ = scal_total(r)
        rhr = rhr + RIDGE * rr
        step = rr / rhr

        quad = []
        for k in range(SLOTS):
            v = x0[k] - step * xq[k]
            quad.append(fold(mu[k] * v * v))
        qvec = (qa, qb, qg[...])
        res1 = (ra - step * qa, rb - step * qb, r0g[...] - step * qg[...])
        scal_send(r + 1, [inner(res1, res1), lanes(sum(quad)), inner(res1, qvec)])
        if final:
            arrive(rxb.at[pl.ds(0, 2 * Z - 1)], rx_sem)
            agb[xy] = sum(rxb[k] for k in range(2 * Z))
            fan(agb.at[xy], ag_sem, xy_dev)
        rr1, curve, cross = scal_total(r + 1)
        beta = rr1 / rr
        curve = curve + RIDGE * rr1 + 2.0 * beta * cross + beta * beta * rhr
        c1 = rr1 / curve
        c0 = step + c1 * beta
        da = c0 * ra + c1 * (ra - step * qa)
        db = c0 * rb + c1 * (rb - step * qb)
        if not final:
            effects = (da, db)
            eg[...] = c0 * r0g[...] + c1 * (r0g[...] - step * qg[...])
        else:
            a_out[...] = effects[0] + da
            b_out[...] = effects[1] + db
            arrive(agb.at[pl.ds(0, XY - 1)], ag_sem)
            for k in range(XY):
                was, res0, img = agb[k, 0], agb[k, 1], agb[k, 2]
                img = img + RIDGE * res0
                g_out[chunk * k : chunk * (k + 1), :] = was + (c0 * res0 + c1 * (res0 - step * img))

def per_device(dims, flows, routing, tile_block, exp_country, imp_country):
    Y, XN, Z = dims
    XY = Y * XN
    chunk = NC // XY
    dma = pltpu.SemaphoreType.DMA
    vmem = functools.partial(pl.BlockSpec, memory_space=pltpu.VMEM)
    smem = functools.partial(pl.BlockSpec, memory_space=pltpu.SMEM)
    cells = SLOTS * SIDE
    pair = (NC, NC)
    sems = [dma((4, 2))] * 4 + [dma((2,))] * 3
    a, b, g = pl.pallas_call(
        functools.partial(kernel, dims),
        out_shape=(
            jax.ShapeDtypeStruct((4, NC), F32),
            jax.ShapeDtypeStruct((8, NC), F32),
            jax.ShapeDtypeStruct(pair, F32),
        ),
        in_specs=[smem(), smem(), pl.BlockSpec(memory_space=pl.ANY), vmem(), vmem()],
        out_specs=(vmem(), vmem(), vmem()),
        scratch_shapes=[
            pltpu.VMEM((SLOTS, SIDE, SIDE), BF16),
            pltpu.VMEM((NC, cells), BF16),
            pltpu.VMEM((cells, NC), BF16),
            pltpu.VMEM((SLOTS, 2 * NC, SIDE), BF16),
            pltpu.VMEM((cells, NC), BF16),
            pltpu.VMEM((SLOTS, SIDE, SIDE), F32),
            pltpu.VMEM((SLOTS, SIDE, SIDE), F32),
            pltpu.VMEM((SLOTS, SIDE, SIDE), F32),
            pltpu.VMEM((cells, 2 * NC), BF16),
            pltpu.VMEM((cells, 2 * NC), BF16),
            pltpu.VMEM((8, NC), F32),
            pltpu.VMEM((8, NC), F32),
            pltpu.VMEM(pair, F32),
            pltpu.VMEM(pair, F32),
            pltpu.VMEM(pair, F32),
            pltpu.VMEM(pair, F32),
            pltpu.VMEM((3,) + pair, F32),
            pltpu.VMEM((4, Z, 8, NC), F32),
            pltpu.VMEM((4, 2 * XY, 8, NC), F32),
            pltpu.VMEM((4, 2, 2, NC), F32),
            pltpu.VMEM((4, 2, Z, 2, NC), F32),
            pltpu.VMEM((4, 2 * XY * Z, NC), F32),
            pltpu.VMEM((XY, 3, chunk, NC), F32),
            pltpu.VMEM((2 * Z, 3, chunk, NC), F32),
            pltpu.VMEM((XY, 3, chunk, NC), F32),
            dma,
        ]
        + sems,
        compiler_params=pltpu.CompilerParams(collective_id=0, has_side_effects=True),
        name="gravity",
    )(
        routing.reshape(-1),
        tile_block,
        flows,
        exp_country.reshape(4, NC),
        imp_country.reshape(8, NC),
    )
    return a.reshape(-1), b.reshape(-1), g


def solution(mesh, xn=4):
    dims = (mesh.shape["exp"] // (2 * xn), xn, mesh.shape["imp"])
    placed = (
        P(("exp", "imp"), None, None),
        P(("exp", "imp"), None, None),
        P(("exp", "imp")),
        P("exp"),
        P("imp"),
    )
    return jax.shard_map(
        functools.partial(per_device, dims),
        mesh=mesh,
        in_specs=placed,
        out_specs=(P("exp"), P("imp"), P()),
        check_vma=False,
    )
```

```python
import functools

import jax
import jax.numpy as jnp
from jax import lax
from jax.experimental import pallas as pl
from jax.experimental.pallas import tpu as pltpu
from jax.sharding import PartitionSpec as P

MESH = pl.DeviceIdType.MESH
RIDGE = 64.0
NC = 128
SIDE = 256
SLOTS = 4
F32 = jnp.float32
BF16 = jnp.bfloat16


def split(x):
    hi = x.astype(BF16)
    lo = (x - hi.astype(F32)).astype(BF16)
    return hi, lo


def dot(x, y):
    return lax.dot_general(x, y, (((1,), (0,)), ((), ())), preferred_element_type=F32)


def dot_nt(x, y):
    return lax.dot_general(x, y, (((1,), (1,)), ((), ())), preferred_element_type=F32)


def hops(off):
    return sum(min(o, 4 - o) for o in off[:3])


def order(offsets):
    return sorted((off for off in offsets if any(off)), key=hops, reverse=True)


def kernel(
    dims,
    routing,
    tile_block,
    flows,
    exp_ids,
    imp_ids,
    a_out,
    b_out,
    g_out,
    fbuf,
    row_t,
    row_s,
    col_t,
    col_s,
    x0,
    xq,
    mu,
    ubuf,
    wbuf,
    vbuf,
    va,
    vb,
    r0g,
    qg,
    eg,
    own,
    tabs,
    image,
    parts,
    gathered,
    zb,
    bb,
    hs,
    hb,
    ps,
    rsb,
    rxb,
    agb,
    fsem,
    z_sem,
    b_sem,
    h_sem,
    p_sem,
    rs_sem,
    rx_sem,
    ag_sem,
    part_sem,
    gath_sem,
):
    Y, XN, Z = dims
    E, XY = 2 * Y * XN, Y * XN
    chunk = NC // XY
    e = lax.axis_index("exp")
    m = lax.axis_index("imp")
    chip = lax.div(e, 2)
    core = lax.rem(e, 2)
    y = lax.div(chip, XN)
    x = lax.rem(chip, XN)
    zc = m * 2 + core

    def device(yy, xx, cc, mm):
        return ((yy * XN + xx) * 2 + cc, mm)

    def step_to(at, off, size):
        return lax.rem(at + off, size) if off else at

    z_dev = [(e, lax.rem(m + k, Z)) for k in range(1, Z)]
    xy_at = [
        (step_to(y, oy, Y), step_to(x, ox, XN)) for oy, ox in order([(i, k) for i in range(Y) for k in range(XN)])
    ]
    xy_dev = [device(yy, xx, core, m) for yy, xx in xy_at]

    def shift(oy, ox, oz, oc):
        return device(step_to(y, oy, Y), step_to(x, ox, XN), 1 - core if oc else core, step_to(m, oz, Z))

    ranges = [(i, k, q, c) for i in range(Y) for k in range(XN) for q in range(Z) for c in range(2)]
    far_dev = [shift(*off) for off in order(ranges) if hops(off) >= 5]
    mid_dev = [shift(*off) for off in order(ranges) if hops(off) == 4]
    near_dev = [shift(*off) for off in order(ranges) if hops(off) <= 3]
    all_dev = far_dev + mid_dev + near_dev
    me = e * Z + m
    own_rows = NC // (E * Z)
    plane_dev = [shift(*off) for off in order([off for off in ranges if off[2] == 0])]
    zc_dev = [
        device(y, x, 1 - core if oc else core, step_to(m, oz, Z))
        for oz, oc in order([(i, k) for i in range(Z) for k in range(2)])
    ]
    after, before = lax.rem(e + 1, E), lax.rem(e + E - 1, E)
    h_dev = [(after, lax.rem(m + k, Z)) for k in range(Z)], [(before, lax.rem(m + k, Z)) for k in range(Z)]
    xy = y * XN + x

    barrier = pltpu.get_barrier_semaphore()
    greet = plane_dev + h_dev[0] + h_dev[1] + zc_dev
    for dev in greet:
        pl.semaphore_signal(barrier, inc=1, device_id=dev, device_id_type=MESH)

    fcopy = pltpu.make_async_copy(flows, fbuf, fsem)
    fcopy.start()

    def push(src, dst, sems, dev):
        pltpu.make_async_remote_copy(
            src_ref=src, dst_ref=dst, send_sem=sems.at[0], recv_sem=sems.at[1], device_id=dev, device_id_type=MESH
        ).start()

    def fan(src, sems, devs):
        for dev in devs:
            push(src, src, sems, dev)

    def arrive(whole, sems):
        for k in (1, 0):
            pltpu.make_async_copy(whole, whole, sems.at[k]).wait()

    riota = lax.broadcasted_iota(jnp.int32, (NC, NC), 0)
    ciota = lax.broadcasted_iota(jnp.int32, (NC, NC), 1)
    riota_f, ciota_f = riota.astype(F32), ciota.astype(F32)
    row_blk, col_blk, live = [], [], []
    for k in range(SLOTS):
        blk = tile_block[k]
        row_blk.append(lax.div(blk, 4))
        col_blk.append(lax.rem(blk, 4))
        hit = jnp.int32(0)
        for t in range(routing.shape[0]):
            hit = hit | jnp.where(routing[t] == k, 1, 0)
        live.append(hit)
    erow = [exp_ids[pl.ds(2 * row_blk[k] + h, 1), :] for k in range(SLOTS) for h in range(2)]
    irow = [imp_ids[pl.ds(2 * col_blk[k] + h, 1), :] for k in range(SLOTS) for h in range(2)]
    ids_t = jnp.concatenate(
        [v.astype(F32) for v in erow + irow] + [jnp.zeros((NC - 4 * SLOTS, NC), F32)], axis=0
    ).T
    for q in range(2 * SLOTS):
        k, h = divmod(q, 2)
        row_t[:, NC * q : NC * (q + 1)] = jnp.where(riota == erow[q], 1.0, 0.0).astype(BF16)
        row_s[NC * q : NC * (q + 1), :] = jnp.where(ciota_f == ids_t[:, q : q + 1], 1.0, 0.0).astype(BF16)
        hot = jnp.where(riota == irow[q], 1.0, 0.0).astype(BF16)
        col_t[k, 0:NC, NC * h : NC * (h + 1)] = hot
        col_t[k, NC : 2 * NC, NC * h : NC * (h + 1)] = hot
        col_s[NC * q : NC * (q + 1), :] = jnp.where(
            ciota_f == ids_t[:, 2 * SLOTS + q : 2 * SLOTS + q + 1], 1.0, 0.0
        ).astype(BF16)
    eids, iids = exp_ids[...].astype(F32), imp_ids[...].astype(F32)

    def least(v):
        return jnp.min(jnp.min(v, axis=0, keepdims=True), axis=1, keepdims=True)

    rf = jnp.broadcast_to(least(eids), (1, NC))
    rl = jnp.broadcast_to(-least(-eids), (1, NC))
    cf = jnp.broadcast_to(least(iids), (1, NC))
    cl = jnp.broadcast_to(-least(-iids), (1, NC))
    lane = lax.broadcasted_iota(jnp.int32, (1, NC), 1).astype(F32)
    zero_row = jnp.zeros((1, NC), F32)
    ends = jnp.concatenate(
        [jnp.where(lane == cf, 1.0, 0.0), jnp.where(lane == cl, 1.0, 0.0)] + [zero_row] * 6, axis=0
    ).astype(BF16)
    ones8 = jnp.ones((8, 2 * NC), BF16)
    row_w = [[jnp.where(row_blk[k] == c, 1.0, 0.0) for c in range(2)] for k in range(SLOTS)]
    col_w = [[jnp.where(col_blk[k] == c, 1.0, 0.0) for c in range(4)] for k in range(SLOTS)]

    def keep(k, v):
        return jnp.where(jnp.full(v.shape, live[k]) > 0, v, 0.0)

    def collect(cells):
        sums = []
        for k in range(SLOTS):
            w = cells(k)
            hi, lo = split(w)
            wbuf[k, :, 0:SIDE] = hi
            wbuf[k, :, SIDE : 2 * SIDE] = lo
            sums.append(jnp.sum(w, axis=0, keepdims=True))
        brows = []
        for c in range(4):
            for h in range(2):
                brows.append(sum(col_w[k][c] * sums[k][:, NC * h : NC * (h + 1)] for k in range(SLOTS)))
        return jnp.concatenate(brows, axis=0)

    def b_send(r, bpart):
        bb[r, e] = bpart
        fan(bb.at[r, e], b_sem.at[r], plane_dev)

    def table_sums():
        for k in range(SLOTS):
            hot = col_s[SIDE * k : SIDE * (k + 1), :]
            vhi, vlo = split(dot(wbuf[k, :, 0:SIDE], hot) + dot(wbuf[k, :, SIDE : 2 * SIDE], hot))
            vbuf[SIDE * k : SIDE * (k + 1), 0:NC] = vhi
            vbuf[SIDE * k : SIDE * (k + 1), NC : 2 * NC] = vlo
        v = vbuf[...]
        wide = dot(row_t[...], v)
        table = wide[:, 0:NC] + wide[:, NC : 2 * NC]
        rsum = dot_nt(ones8, v)
        arows = []
        for c in range(2):
            for h in range(2):
                arows.append(
                    sum(
                        row_w[k][c] * rsum[0:1, SIDE * k + NC * h : SIDE * k + NC * (h + 1)]
                        for k in range(SLOTS)
                    )
                )
        return table, arows

    def table_send(r, table, arows):
        first = jnp.sum(jnp.where(riota_f == rf, table, 0.0), axis=0, keepdims=True)
        last = jnp.sum(jnp.where(riota_f == rl, table, 0.0), axis=0, keepdims=True)
        hs[r, 0] = jnp.concatenate([last, rl], axis=0)
        hs[r, 1] = jnp.concatenate([first, rf], axis=0)
        for side in range(2):
            for dev in h_dev[side]:
                push(hs.at[r, side], hb.at[r, side, m], h_sem.at[r], dev)
        hi, lo = split(table)
        edge = dot_nt(ends, jnp.concatenate([hi, lo], axis=0))
        edge = edge[:, 0:NC] + edge[:, NC : 2 * NC]
        zb[r, m] = jnp.concatenate(arows + [edge[0:1], edge[1:2], cf, cl], axis=0)
        fan(zb.at[r, m], z_sem.at[r], z_dev)

    def scal_store(s, rows):
        rows = jnp.sum(jnp.concatenate(rows + [zero_row] * (8 - len(rows)), axis=0), axis=1, keepdims=True)
        ps[s, pl.ds(me, 1), :] = sum(jnp.where(lane == float(k), rows[k : k + 1], 0.0) for k in range(3))

    def scal_fan(s, devs):
        fan(ps.at[s, pl.ds(me, 1)], p_sem.at[s], devs)

    def scal_total(s):
        arrive(ps.at[s, pl.ds(0, E * Z - 1)], p_sem.at[s])
        total = jnp.sum(ps[s], axis=0, keepdims=True)
        return [total[:, k : k + 1] for k in range(3)]

    def columns(r, avec):
        va[0:4, :] = avec
        tiles = [va[pl.ds(2 * row_blk[k] + h, 1), :] for k in range(SLOTS) for h in range(2)]
        prev = zb[r, lax.rem(m + Z - 1, Z), 5:6, :]
        nxt = zb[r, lax.rem(m + 1, Z), 4:5, :]
        return jnp.concatenate(tiles + [prev, nxt, jnp.zeros((NC - 10, NC), F32)], axis=0).T

    def table_end(r, table, cols):
        cl_prev = zb[r, lax.rem(m + Z - 1, Z), 7:8, :]
        cf_next = zb[r, lax.rem(m + 1, Z), 6:7, :]
        table = table + jnp.where(ciota_f == cl_prev, cols[:, 8:9], 0.0)
        table = table + jnp.where(ciota_f == cf_next, cols[:, 9:10], 0.0)
        arrive(hb.at[r], h_sem.at[r])
        from_prev, from_next = (sum(hb[r, side, k] for k in range(Z)) for side in range(2))
        rl_prev, rf_next = hb[r, 0, 0, 1:2, :], hb[r, 1, 0, 1:2, :]
        table = table + jnp.where(riota_f == rl_prev, from_prev[0:1], 0.0)
        table = table + jnp.where(riota_f == rf_next, from_next[0:1], 0.0)
        if r == 0:
            skip_r = jnp.where(rl_prev == rf, 1.0, 0.0)
            skip_c = jnp.where(cl_prev == cf, 1.0, 0.0)
            mine = (riota_f >= rf + skip_r) & (riota_f <= rl) & (ciota_f >= cf + skip_c) & (ciota_f <= cl)
            own[...] = jnp.where(mine, 1.0, 0.0)
        return table

    def z_end(r):
        arrive(zb.at[r, pl.ds(0, Z - 1)], z_sem.at[r])
        return sum(zb[r, k, 0:4, :] for k in range(Z))

    def b_end(r):
        arrive(bb.at[r, pl.ds(0, E - 1)], b_sem.at[r])
        return sum(bb[r, k] for k in range(E))

    def select(gval):
        hi, lo = split(gval)
        ubuf[...] = dot(row_s[...], jnp.concatenate([hi, lo], axis=1)).astype(BF16)

    def expand(cols, bvec):
        vb[...] = bvec

        def tile(k):
            brow = jnp.concatenate([vb[pl.ds(2 * col_blk[k] + h, 1), :] for h in range(2)], axis=1)
            acol = jnp.concatenate([cols[:, 2 * k + h : 2 * k + h + 1] for h in range(2)], axis=0)
            return dot(ubuf[SIDE * k : SIDE * (k + 1), :], col_t[k]) + acol + brow

        return tile

    def fold(v):
        v = jnp.sum(v.reshape(SIDE // 8, 8, SIDE), axis=0)
        return v[:, 0:NC] + v[:, NC:SIDE]

    def lanes(v):
        return jnp.sum(v, axis=0, keepdims=True)

    def inner(u, v):
        total = lanes(u[0] * v[0]) * (1.0 / Z) + lanes(u[1] * v[1]) * (1.0 / E)
        return total + lanes(own[...] * u[2] * v[2])

    def scatter():
        rsb[xy] = tabs[:, pl.ds(xy * chunk, chunk), :]
        for (yy, xx), dev in zip(xy_at, xy_dev):
            push(tabs.at[:, pl.ds((yy * XN + xx) * chunk, chunk)], rsb.at[xy], rs_sem, dev)

    def rows_out():
        parts[pl.ds(me * own_rows, own_rows), :] = image[pl.ds(me * own_rows, own_rows), :]
        for ee, mm in all_dev:
            src = image.at[pl.ds((ee * Z + mm) * own_rows, own_rows)]
            push(src, parts.at[pl.ds(me * own_rows, own_rows)], part_sem, (ee, mm))

    def rows_back():
        arrive(parts.at[pl.ds(0, NC - own_rows)], part_sem)
        gathered[pl.ds(me * own_rows, own_rows), :] = jnp.sum(
            parts[...].reshape(E * Z, own_rows, NC), axis=0
        ) if own_rows > 1 else jnp.sum(parts[...], axis=0, keepdims=True)
        fan(gathered.at[pl.ds(me * own_rows, own_rows)], gath_sem, all_dev)

    effects = None
    for newton in range(2):
        final = newton == 1
        r = 2 * newton
        if not final:

            def cells(k):
                mu[k] = keep(k, jnp.ones((SIDE, SIDE), F32))
                return keep(k, fbuf[k].astype(F32) - 1.0)

            fcopy.wait()
        else:

            def cells(k):
                rate = keep(k, jnp.exp(c0 * x0[k] + c1 * (x0[k] - step * xq[k])))
                mu[k] = rate
                return keep(k, fbuf[k].astype(F32)) - rate

        bpart = collect(cells)
        if not final:
            pl.semaphore_wait(barrier, len(greet))
        b_send(r, bpart)
        table, arows = table_sums()
        table_send(r, table, arows)
        if final:
            tabs[0] = eg[...] * own[...]
            tabs[1] = table
            scatter()
        ra = z_end(r)
        if final:
            ra = ra - RIDGE * effects[0]
        cols = columns(r, ra)
        rg = table_end(r, table, cols)
        if final:
            rg = rg - RIDGE * eg[...]
        r0g[...] = rg
        select(rg)
        rb = b_end(r)
        if final:
            rb = rb - RIDGE * effects[1]
        res = (ra, rb, rg)
        tile = expand(cols, rb)
        quad = []

        def cells(k):
            v = tile(k)
            x0[k] = v
            w = mu[k] * v
            quad.append(fold(w * v))
            return w

        bpart = collect(cells)
        scal_store(r, [inner(res, res), lanes(sum(quad))])
        scal_fan(r, far_dev)
        b_send(r + 1, bpart)
        scal_fan(r, mid_dev)
        table, arows = table_sums()
        table_send(r + 1, table, arows)
        scal_fan(r, near_dev)
        if final:
            arrive(rsb.at[pl.ds(0, XY - 1)], rs_sem)
            rxb[zc] = sum(rsb[k] for k in range(XY))
            fan(rxb.at[zc], rx_sem, zc_dev)
            image[...] = table
            rows_out()
        qa = z_end(r + 1) + RIDGE * ra
        cols = columns(r + 1, qa)
        qgv = table_end(r + 1, table, cols) + RIDGE * r0g[...]
        qg[...] = qgv
        select(qgv)
        qb = b_end(r + 1) + RIDGE * rb
        tile = expand(cols, qb)
        for k in range(SLOTS):
            xq[k] = tile(k)
        rr, rhr, _ = scal_total(r)
        rhr = rhr + RIDGE * rr
        step = rr / rhr

        quad = []
        for k in range(SLOTS):
            v = x0[k] - step * xq[k]
            quad.append(fold(mu[k] * v * v))
        qvec = (qa, qb, qg[...])
        res1 = (ra - step * qa, rb - step * qb, r0g[...] - step * qg[...])
        scal_store(r + 1, [inner(res1, res1), lanes(sum(quad)), inner(res1, qvec)])
        scal_fan(r + 1, all_dev)
        if final:
            rows_back()
            arrive(rxb.at[pl.ds(0, 2 * Z - 1)], rx_sem)
            agb[xy] = sum(rxb[k] for k in range(2 * Z))
            fan(agb.at[xy], ag_sem, xy_dev)
        rr1, curve, cross = scal_total(r + 1)
        beta = rr1 / rr
        curve = curve + RIDGE * rr1 + 2.0 * beta * cross + beta * beta * rhr
        c1 = rr1 / curve
        c0 = step + c1 * beta
        da = c0 * ra + c1 * (ra - step * qa)
        db = c0 * rb + c1 * (rb - step * qb)
        if not final:
            effects = (da, db)
            eg[...] = c0 * r0g[...] + c1 * (r0g[...] - step * qg[...])
        else:
            a_out[...] = effects[0] + da
            b_out[...] = effects[1] + db
            arrive(agb.at[pl.ds(0, XY - 1)], ag_sem)
            arrive(gathered.at[pl.ds(0, NC - own_rows)], gath_sem)
            for k in range(XY):
                was = agb[k, 0]
                res0 = agb[k, 1] - RIDGE * was
                img = gathered[chunk * k : chunk * (k + 1), :] + RIDGE * res0
                g_out[chunk * k : chunk * (k + 1), :] = was + (c0 * res0 + c1 * (res0 - step * img))

def publish(a, b, g, a_out, b_out, g_out):
    a_out[...] = a[...]
    b_out[...] = b[...]
    g_out[...] = g[...]


def per_device(dims, flows, routing, tile_block, exp_country, imp_country):
    Y, XN, Z = dims
    XY = Y * XN
    chunk = NC // XY
    dma = pltpu.SemaphoreType.DMA
    vmem = functools.partial(pl.BlockSpec, memory_space=pltpu.VMEM)
    smem = functools.partial(pl.BlockSpec, memory_space=pltpu.SMEM)
    cells = SLOTS * SIDE
    pair = (NC, NC)
    sems = [dma((4, 2))] * 4 + [dma((2,))] * 5
    a, b, g = pl.pallas_call(
        functools.partial(kernel, dims),
        out_shape=(
            jax.ShapeDtypeStruct((4, NC), F32),
            jax.ShapeDtypeStruct((8, NC), F32),
            jax.ShapeDtypeStruct(pair, F32),
        ),
        in_specs=[smem(), smem(), pl.BlockSpec(memory_space=pl.ANY), vmem(), vmem()],
        out_specs=(vmem(), vmem(), vmem()),
        scratch_shapes=[
            pltpu.VMEM((SLOTS, SIDE, SIDE), BF16),
            pltpu.VMEM((NC, cells), BF16),
            pltpu.VMEM((cells, NC), BF16),
            pltpu.VMEM((SLOTS, 2 * NC, SIDE), BF16),
            pltpu.VMEM((cells, NC), BF16),
            pltpu.VMEM((SLOTS, SIDE, SIDE), F32),
            pltpu.VMEM((SLOTS, SIDE, SIDE), F32),
            pltpu.VMEM((SLOTS, SIDE, SIDE), F32),
            pltpu.VMEM((cells, 2 * NC), BF16),
            pltpu.VMEM((SLOTS, SIDE, 2 * SIDE), BF16),
            pltpu.VMEM((cells, 2 * NC), BF16),
            pltpu.VMEM((8, NC), F32),
            pltpu.VMEM((8, NC), F32),
            pltpu.VMEM(pair, F32),
            pltpu.VMEM(pair, F32),
            pltpu.VMEM(pair, F32),
            pltpu.VMEM(pair, F32),
            pltpu.VMEM((2,) + pair, F32),
            pltpu.VMEM(pair, F32),
            pltpu.VMEM(pair, F32),
            pltpu.VMEM(pair, F32),
            pltpu.VMEM((4, Z, 8, NC), F32),
            pltpu.VMEM((4, 2 * XY, 8, NC), F32),
            pltpu.VMEM((4, 2, 2, NC), F32),
            pltpu.VMEM((4, 2, Z, 2, NC), F32),
            pltpu.VMEM((4, 2 * XY * Z, NC), F32),
            pltpu.VMEM((XY, 2, chunk, NC), F32),
            pltpu.VMEM((2 * Z, 2, chunk, NC), F32),
            pltpu.VMEM((XY, 2, chunk, NC), F32),
            dma,
        ]
        + sems,
        compiler_params=pltpu.CompilerParams(collective_id=0, has_side_effects=True),
        name="gravity",
    )(
        routing.reshape(-1),
        tile_block,
        flows,
        exp_country.reshape(4, NC),
        imp_country.reshape(8, NC),
    )
    a, b, g = pl.pallas_call(
        publish,
        out_shape=(
            jax.ShapeDtypeStruct((4, NC), F32),
            jax.ShapeDtypeStruct((8, NC), F32),
            jax.ShapeDtypeStruct(pair, F32),
        ),
        in_specs=[vmem()] * 3,
        out_specs=(vmem(), vmem(), vmem()),
        name="publish",
    )(a, b, g)
    return a.reshape(-1), b.reshape(-1), g


def solution(mesh, xn=4):
    dims = (mesh.shape["exp"] // (2 * xn), xn, mesh.shape["imp"])
    placed = (
        P(("exp", "imp"), None, None),
        P(("exp", "imp"), None, None),
        P(("exp", "imp")),
        P("exp"),
        P("imp"),
    )
    return jax.shard_map(
        functools.partial(per_device, dims),
        mesh=mesh,
        in_specs=placed,
        out_specs=(P("exp"), P("imp"), P()),
        check_vma=False,
    )
```

```python
import functools

import jax
import jax.numpy as jnp
from jax import lax
from jax.experimental import pallas as pl
from jax.experimental.pallas import tpu as pltpu
from jax.sharding import PartitionSpec as P

MESH = pl.DeviceIdType.MESH
RIDGE = 64.0
NC = 128
SIDE = 256
SLOTS = 4
F32 = jnp.float32
BF16 = jnp.bfloat16


def split(x):
    hi = x.astype(BF16)
    lo = (x - hi.astype(F32)).astype(BF16)
    return hi, lo


def dot(x, y):
    return lax.dot_general(x, y, (((1,), (0,)), ((), ())), preferred_element_type=F32)


def dot_nt(x, y):
    return lax.dot_general(x, y, (((1,), (1,)), ((), ())), preferred_element_type=F32)


def hops(off):
    return sum(min(o, 4 - o) for o in off[:3])


def order(offsets):
    return sorted((off for off in offsets if any(off)), key=hops, reverse=True)


def kernel(
    dims,
    routing,
    tile_block,
    flows,
    exp_ids,
    imp_ids,
    a_out,
    b_out,
    g_out,
    fbuf,
    row_t,
    row_s,
    col_t,
    col_s,
    x0,
    xq,
    mu,
    ubuf,
    wbuf,
    vbuf,
    va,
    vb,
    r0g,
    qg,
    eg,
    own,
    tabs,
    image,
    parts,
    gathered,
    zb,
    bb,
    hs,
    hb,
    ps,
    rsb,
    rxb,
    agb,
    fsem,
    z_sem,
    b_sem,
    h_sem,
    p_sem,
    rs_sem,
    rx_sem,
    ag_sem,
    part_sem,
    gath_sem,
):
    Y, XN, Z = dims
    E, XY = 2 * Y * XN, Y * XN
    chunk = NC // XY
    e = lax.axis_index("exp")
    m = lax.axis_index("imp")
    chip = lax.div(e, 2)
    core = lax.rem(e, 2)
    y = lax.div(chip, XN)
    x = lax.rem(chip, XN)
    zc = m * 2 + core

    def device(yy, xx, cc, mm):
        return ((yy * XN + xx) * 2 + cc, mm)

    def step_to(at, off, size):
        return lax.rem(at + off, size) if off else at

    z_dev = [(e, lax.rem(m + k, Z)) for k in range(1, Z)]
    xy_at = [
        (step_to(y, oy, Y), step_to(x, ox, XN)) for oy, ox in order([(i, k) for i in range(Y) for k in range(XN)])
    ]
    xy_dev = [device(yy, xx, core, m) for yy, xx in xy_at]

    def shift(oy, ox, oz, oc):
        return device(step_to(y, oy, Y), step_to(x, ox, XN), 1 - core if oc else core, step_to(m, oz, Z))

    ranges = [(i, k, q, c) for i in range(Y) for k in range(XN) for q in range(Z) for c in range(2)]
    far_dev = [shift(*off) for off in order(ranges) if hops(off) >= 5]
    mid_dev = [shift(*off) for off in order(ranges) if hops(off) == 4]
    near_dev = [shift(*off) for off in order(ranges) if hops(off) <= 3]
    all_dev = far_dev + mid_dev + near_dev
    me = e * Z + m
    own_rows = NC // (E * Z)
    plane_dev = [shift(*off) for off in order([off for off in ranges if off[2] == 0])]
    zc_dev = [
        device(y, x, 1 - core if oc else core, step_to(m, oz, Z))
        for oz, oc in order([(i, k) for i in range(Z) for k in range(2)])
    ]
    after, before = lax.rem(e + 1, E), lax.rem(e + E - 1, E)
    h_dev = [(after, lax.rem(m + k, Z)) for k in range(Z)], [(before, lax.rem(m + k, Z)) for k in range(Z)]
    xy = y * XN + x

    barrier = pltpu.get_barrier_semaphore()
    greet = plane_dev + h_dev[0] + h_dev[1] + zc_dev
    for dev in greet:
        pl.semaphore_signal(barrier, inc=1, device_id=dev, device_id_type=MESH)

    fcopy = pltpu.make_async_copy(flows, fbuf, fsem)
    fcopy.start()

    def push(src, dst, sems, dev):
        pltpu.make_async_remote_copy(
            src_ref=src, dst_ref=dst, send_sem=sems.at[0], recv_sem=sems.at[1], device_id=dev, device_id_type=MESH
        ).start()

    def fan(src, sems, devs):
        for dev in devs:
            push(src, src, sems, dev)

    def arrive(whole, sems):
        for k in (1, 0):
            pltpu.make_async_copy(whole, whole, sems.at[k]).wait()

    riota = lax.broadcasted_iota(jnp.int32, (NC, NC), 0)
    ciota = lax.broadcasted_iota(jnp.int32, (NC, NC), 1)
    riota_f, ciota_f = riota.astype(F32), ciota.astype(F32)
    row_blk, col_blk, live = [], [], []
    for k in range(SLOTS):
        blk = tile_block[k]
        row_blk.append(lax.div(blk, 4))
        col_blk.append(lax.rem(blk, 4))
        hit = jnp.int32(0)
        for t in range(routing.shape[0]):
            hit = hit | jnp.where(routing[t] == k, 1, 0)
        live.append(hit)
    erow = [exp_ids[pl.ds(2 * row_blk[k] + h, 1), :] for k in range(SLOTS) for h in range(2)]
    irow = [imp_ids[pl.ds(2 * col_blk[k] + h, 1), :] for k in range(SLOTS) for h in range(2)]
    ids_t = jnp.concatenate(
        [v.astype(F32) for v in erow + irow] + [jnp.zeros((NC - 4 * SLOTS, NC), F32)], axis=0
    ).T
    for q in range(2 * SLOTS):
        k, h = divmod(q, 2)
        row_t[:, NC * q : NC * (q + 1)] = jnp.where(riota == erow[q], 1.0, 0.0).astype(BF16)
        row_s[NC * q : NC * (q + 1), :] = jnp.where(ciota_f == ids_t[:, q : q + 1], 1.0, 0.0).astype(BF16)
        hot = jnp.where(riota == irow[q], 1.0, 0.0).astype(BF16)
        col_t[k, 0:NC, NC * h : NC * (h + 1)] = hot
        col_t[k, NC : 2 * NC, NC * h : NC * (h + 1)] = hot
        col_s[NC * q : NC * (q + 1), :] = jnp.where(
            ciota_f == ids_t[:, 2 * SLOTS + q : 2 * SLOTS + q + 1], 1.0, 0.0
        ).astype(BF16)
    eids, iids = exp_ids[...].astype(F32), imp_ids[...].astype(F32)

    def least(v):
        return jnp.min(jnp.min(v, axis=0, keepdims=True), axis=1, keepdims=True)

    rf = jnp.broadcast_to(least(eids), (1, NC))
    rl = jnp.broadcast_to(-least(-eids), (1, NC))
    cf = jnp.broadcast_to(least(iids), (1, NC))
    cl = jnp.broadcast_to(-least(-iids), (1, NC))
    lane = lax.broadcasted_iota(jnp.int32, (1, NC), 1).astype(F32)
    zero_row = jnp.zeros((1, NC), F32)
    ends = jnp.concatenate(
        [jnp.where(lane == cf, 1.0, 0.0), jnp.where(lane == cl, 1.0, 0.0)] + [zero_row] * 6, axis=0
    ).astype(BF16)
    ones8 = jnp.ones((8, 2 * NC), BF16)
    row_w = [[jnp.where(row_blk[k] == c, 1.0, 0.0) for c in range(2)] for k in range(SLOTS)]
    col_w = [[jnp.where(col_blk[k] == c, 1.0, 0.0) for c in range(4)] for k in range(SLOTS)]

    def keep(k, v):
        return jnp.where(jnp.full(v.shape, live[k]) > 0, v, 0.0)

    def collect(cells):
        sums = []
        for k in range(SLOTS):
            w = cells(k)
            hi, lo = split(w)
            wbuf[k, :, 0:SIDE] = hi
            wbuf[k, :, SIDE : 2 * SIDE] = lo
            sums.append(jnp.sum(w, axis=0, keepdims=True))
        brows = []
        for c in range(4):
            for h in range(2):
                brows.append(sum(col_w[k][c] * sums[k][:, NC * h : NC * (h + 1)] for k in range(SLOTS)))
        return jnp.concatenate(brows, axis=0)

    def b_store(r, bpart):
        bb[r, e] = bpart

    def b_send(r):
        fan(bb.at[r, e], b_sem.at[r], plane_dev)

    def table_sums():
        for k in range(SLOTS):
            hot = col_s[SIDE * k : SIDE * (k + 1), :]
            vhi, vlo = split(dot(wbuf[k, :, 0:SIDE], hot) + dot(wbuf[k, :, SIDE : 2 * SIDE], hot))
            vbuf[SIDE * k : SIDE * (k + 1), 0:NC] = vhi
            vbuf[SIDE * k : SIDE * (k + 1), NC : 2 * NC] = vlo
        v = vbuf[...]
        wide = dot(row_t[...], v)
        table = wide[:, 0:NC] + wide[:, NC : 2 * NC]
        rsum = dot_nt(ones8, v)
        arows = []
        for c in range(2):
            for h in range(2):
                arows.append(
                    sum(
                        row_w[k][c] * rsum[0:1, SIDE * k + NC * h : SIDE * k + NC * (h + 1)]
                        for k in range(SLOTS)
                    )
                )
        return table, arows

    def table_store(r, table, arows):
        first = jnp.sum(jnp.where(riota_f == rf, table, 0.0), axis=0, keepdims=True)
        last = jnp.sum(jnp.where(riota_f == rl, table, 0.0), axis=0, keepdims=True)
        hs[r, 0] = jnp.concatenate([last, rl], axis=0)
        hs[r, 1] = jnp.concatenate([first, rf], axis=0)

    def rows_send(r):
        for side in range(2):
            for dev in h_dev[side]:
                push(hs.at[r, side], hb.at[r, side, m], h_sem.at[r], dev)

    def edge_store(r, table, arows):
        hi, lo = split(table)
        edge = dot_nt(ends, jnp.concatenate([hi, lo], axis=0))
        edge = edge[:, 0:NC] + edge[:, NC : 2 * NC]
        zb[r, m] = jnp.concatenate(arows + [edge[0:1], edge[1:2], cf, cl], axis=0)

    def edge_send(r):
        fan(zb.at[r, m], z_sem.at[r], z_dev)

    def table_send(r, table, arows):
        table_store(r, table, arows)
        rows_send(r)
        edge_store(r, table, arows)
        edge_send(r)

    def scal_store(s, rows):
        rows = jnp.sum(jnp.concatenate(rows + [zero_row] * (8 - len(rows)), axis=0), axis=1, keepdims=True)
        ps[s, pl.ds(me, 1), :] = sum(jnp.where(lane == float(k), rows[k : k + 1], 0.0) for k in range(3))

    def scal_fan(s, devs):
        fan(ps.at[s, pl.ds(me, 1)], p_sem.at[s], devs)

    def scal_total(s):
        arrive(ps.at[s, pl.ds(0, E * Z - 1)], p_sem.at[s])
        total = jnp.sum(ps[s], axis=0, keepdims=True)
        return [total[:, k : k + 1] for k in range(3)]

    def columns(r, avec):
        va[0:4, :] = avec
        tiles = [va[pl.ds(2 * row_blk[k] + h, 1), :] for k in range(SLOTS) for h in range(2)]
        prev = zb[r, lax.rem(m + Z - 1, Z), 5:6, :]
        nxt = zb[r, lax.rem(m + 1, Z), 4:5, :]
        return jnp.concatenate(tiles + [prev, nxt, jnp.zeros((NC - 10, NC), F32)], axis=0).T

    def table_end(r, table, cols):
        cl_prev = zb[r, lax.rem(m + Z - 1, Z), 7:8, :]
        cf_next = zb[r, lax.rem(m + 1, Z), 6:7, :]
        table = table + jnp.where(ciota_f == cl_prev, cols[:, 8:9], 0.0)
        table = table + jnp.where(ciota_f == cf_next, cols[:, 9:10], 0.0)
        arrive(hb.at[r], h_sem.at[r])
        from_prev, from_next = (sum(hb[r, side, k] for k in range(Z)) for side in range(2))
        rl_prev, rf_next = hb[r, 0, 0, 1:2, :], hb[r, 1, 0, 1:2, :]
        table = table + jnp.where(riota_f == rl_prev, from_prev[0:1], 0.0)
        table = table + jnp.where(riota_f == rf_next, from_next[0:1], 0.0)
        if r == 0:
            skip_r = jnp.where(rl_prev == rf, 1.0, 0.0)
            skip_c = jnp.where(cl_prev == cf, 1.0, 0.0)
            mine = (riota_f >= rf + skip_r) & (riota_f <= rl) & (ciota_f >= cf + skip_c) & (ciota_f <= cl)
            own[...] = jnp.where(mine, 1.0, 0.0)
        return table

    def z_end(r):
        arrive(zb.at[r, pl.ds(0, Z - 1)], z_sem.at[r])
        return sum(zb[r, k, 0:4, :] for k in range(Z))

    def b_end(r):
        arrive(bb.at[r, pl.ds(0, E - 1)], b_sem.at[r])
        return sum(bb[r, k] for k in range(E))

    def select(gval):
        hi, lo = split(gval)
        ubuf[...] = dot(row_s[...], jnp.concatenate([hi, lo], axis=1)).astype(BF16)

    def expand(cols, bvec):
        vb[...] = bvec

        def tile(k):
            brow = jnp.concatenate([vb[pl.ds(2 * col_blk[k] + h, 1), :] for h in range(2)], axis=1)
            acol = jnp.concatenate([cols[:, 2 * k + h : 2 * k + h + 1] for h in range(2)], axis=0)
            return dot(ubuf[SIDE * k : SIDE * (k + 1), :], col_t[k]) + acol + brow

        return tile

    def fold(v):
        v = jnp.sum(v.reshape(SIDE // 8, 8, SIDE), axis=0)
        return v[:, 0:NC] + v[:, NC:SIDE]

    def lanes(v):
        return jnp.sum(v, axis=0, keepdims=True)

    def inner(u, v):
        total = lanes(u[0] * v[0]) * (1.0 / Z) + lanes(u[1] * v[1]) * (1.0 / E)
        return total + lanes(own[...] * u[2] * v[2])

    def scatter():
        rsb[xy] = tabs[:, pl.ds(xy * chunk, chunk), :]
        for (yy, xx), dev in zip(xy_at, xy_dev):
            push(tabs.at[:, pl.ds((yy * XN + xx) * chunk, chunk)], rsb.at[xy], rs_sem, dev)

    def rows_out():
        parts[pl.ds(me * own_rows, own_rows), :] = image[pl.ds(me * own_rows, own_rows), :]
        for ee, mm in all_dev:
            src = image.at[pl.ds((ee * Z + mm) * own_rows, own_rows)]
            push(src, parts.at[pl.ds(me * own_rows, own_rows)], part_sem, (ee, mm))

    def rows_back():
        arrive(parts.at[pl.ds(0, NC - own_rows)], part_sem)
        gathered[pl.ds(me * own_rows, own_rows), :] = jnp.sum(
            parts[...].reshape(E * Z, own_rows, NC), axis=0
        ) if own_rows > 1 else jnp.sum(parts[...], axis=0, keepdims=True)
        fan(gathered.at[pl.ds(me * own_rows, own_rows)], gath_sem, all_dev)

    effects = None
    for newton in range(2):
        final = newton == 1
        r = 2 * newton
        if not final:

            def cells(k):
                mu[k] = keep(k, jnp.ones((SIDE, SIDE), F32))
                return keep(k, fbuf[k].astype(F32) - 1.0)

            fcopy.wait()
        else:

            def cells(k):
                rate = keep(k, jnp.exp(c0 * x0[k] + c1 * (x0[k] - step * xq[k])))
                mu[k] = rate
                return keep(k, fbuf[k].astype(F32)) - rate

        bpart = collect(cells)
        b_store(r, bpart)
        if not final:
            table, arows = table_sums()
            table_store(r, table, arows)
            edge_store(r, table, arows)
            pl.semaphore_wait(barrier, len(greet))
            b_send(r)
            rows_send(r)
            edge_send(r)
        else:
            b_send(r)
            table, arows = table_sums()
            table_send(r, table, arows)
        if final:
            tabs[0] = eg[...] * own[...]
            tabs[1] = table
            scatter()
        ra = z_end(r)
        if final:
            ra = ra - RIDGE * effects[0]
        cols = columns(r, ra)
        rg = table_end(r, table, cols)
        if final:
            rg = rg - RIDGE * eg[...]
        r0g[...] = rg
        select(rg)
        rb = b_end(r)
        if final:
            rb = rb - RIDGE * effects[1]
        res = (ra, rb, rg)
        tile = expand(cols, rb)
        quad = []

        def cells(k):
            v = tile(k)
            x0[k] = v
            w = mu[k] * v
            quad.append(fold(w * v))
            return w

        bpart = collect(cells)
        scal_store(r, [inner(res, res), lanes(sum(quad))])
        scal_fan(r, far_dev)
        b_store(r + 1, bpart)
        b_send(r + 1)
        scal_fan(r, mid_dev)
        table, arows = table_sums()
        table_send(r + 1, table, arows)
        scal_fan(r, near_dev)
        if final:
            arrive(rsb.at[pl.ds(0, XY - 1)], rs_sem)
            rxb[zc] = sum(rsb[k] for k in range(XY))
            fan(rxb.at[zc], rx_sem, zc_dev)
            image[...] = table
            rows_out()
        qa = z_end(r + 1) + RIDGE * ra
        cols = columns(r + 1, qa)
        qgv = table_end(r + 1, table, cols) + RIDGE * r0g[...]
        qg[...] = qgv
        select(qgv)
        qb = b_end(r + 1) + RIDGE * rb
        tile = expand(cols, qb)
        for k in range(SLOTS):
            xq[k] = tile(k)
        rr, rhr, _ = scal_total(r)
        rhr = rhr + RIDGE * rr
        step = rr / rhr

        quad = []
        for k in range(SLOTS):
            v = x0[k] - step * xq[k]
            quad.append(fold(mu[k] * v * v))
        qvec = (qa, qb, qg[...])
        res1 = (ra - step * qa, rb - step * qb, r0g[...] - step * qg[...])
        scal_store(r + 1, [inner(res1, res1), lanes(sum(quad)), inner(res1, qvec)])
        scal_fan(r + 1, all_dev)
        if final:
            rows_back()
            arrive(rxb.at[pl.ds(0, 2 * Z - 1)], rx_sem)
            agb[xy] = sum(rxb[k] for k in range(2 * Z))
            fan(agb.at[xy], ag_sem, xy_dev)
        rr1, curve, cross = scal_total(r + 1)
        beta = rr1 / rr
        curve = curve + RIDGE * rr1 + 2.0 * beta * cross + beta * beta * rhr
        c1 = rr1 / curve
        c0 = step + c1 * beta
        da = c0 * ra + c1 * (ra - step * qa)
        db = c0 * rb + c1 * (rb - step * qb)
        if not final:
            effects = (da, db)
            eg[...] = c0 * r0g[...] + c1 * (r0g[...] - step * qg[...])
        else:
            a_out[...] = effects[0] + da
            b_out[...] = effects[1] + db
            arrive(agb.at[pl.ds(0, XY - 1)], ag_sem)
            arrive(gathered.at[pl.ds(0, NC - own_rows)], gath_sem)
            for k in range(XY):
                was = agb[k, 0]
                res0 = agb[k, 1] - RIDGE * was
                img = gathered[chunk * k : chunk * (k + 1), :] + RIDGE * res0
                g_out[chunk * k : chunk * (k + 1), :] = was + (c0 * res0 + c1 * (res0 - step * img))

def publish(a, b, g, a_out, b_out, g_out, sems):
    copies = [pltpu.make_async_copy(src, dst, sems.at[k]) for k, (src, dst) in enumerate(((g, g_out), (a, a_out), (b, b_out)))]
    for copy in copies:
        copy.start()
    for copy in copies:
        copy.wait()


def per_device(dims, flows, routing, tile_block, exp_country, imp_country):
    Y, XN, Z = dims
    XY = Y * XN
    chunk = NC // XY
    dma = pltpu.SemaphoreType.DMA
    vmem = functools.partial(pl.BlockSpec, memory_space=pltpu.VMEM)
    smem = functools.partial(pl.BlockSpec, memory_space=pltpu.SMEM)
    cells = SLOTS * SIDE
    pair = (NC, NC)
    sems = [dma((4, 2))] * 4 + [dma((2,))] * 5
    a, b, g = pl.pallas_call(
        functools.partial(kernel, dims),
        out_shape=(pltpu.VMEM((4, NC), F32), pltpu.VMEM((8, NC), F32), pltpu.VMEM(pair, F32)),
        in_specs=[smem(), smem(), pl.BlockSpec(memory_space=pl.ANY), vmem(), vmem()],
        out_specs=(vmem(), vmem(), vmem()),
        scratch_shapes=[
            pltpu.VMEM((SLOTS, SIDE, SIDE), BF16),
            pltpu.VMEM((NC, cells), BF16),
            pltpu.VMEM((cells, NC), BF16),
            pltpu.VMEM((SLOTS, 2 * NC, SIDE), BF16),
            pltpu.VMEM((cells, NC), BF16),
            pltpu.VMEM((SLOTS, SIDE, SIDE), F32),
            pltpu.VMEM((SLOTS, SIDE, SIDE), F32),
            pltpu.VMEM((SLOTS, SIDE, SIDE), F32),
            pltpu.VMEM((cells, 2 * NC), BF16),
            pltpu.VMEM((SLOTS, SIDE, 2 * SIDE), BF16),
            pltpu.VMEM((cells, 2 * NC), BF16),
            pltpu.VMEM((8, NC), F32),
            pltpu.VMEM((8, NC), F32),
            pltpu.VMEM(pair, F32),
            pltpu.VMEM(pair, F32),
            pltpu.VMEM(pair, F32),
            pltpu.VMEM(pair, F32),
            pltpu.VMEM((2,) + pair, F32),
            pltpu.VMEM(pair, F32),
            pltpu.VMEM(pair, F32),
            pltpu.VMEM(pair, F32),
            pltpu.VMEM((4, Z, 8, NC), F32),
            pltpu.VMEM((4, 2 * XY, 8, NC), F32),
            pltpu.VMEM((4, 2, 2, NC), F32),
            pltpu.VMEM((4, 2, Z, 2, NC), F32),
            pltpu.VMEM((4, 2 * XY * Z, NC), F32),
            pltpu.VMEM((XY, 2, chunk, NC), F32),
            pltpu.VMEM((2 * Z, 2, chunk, NC), F32),
            pltpu.VMEM((XY, 2, chunk, NC), F32),
            dma,
        ]
        + sems,
        compiler_params=pltpu.CompilerParams(collective_id=0, has_side_effects=True),
        name="gravity",
    )(
        routing.reshape(-1),
        tile_block,
        flows,
        exp_country.reshape(4, NC),
        imp_country.reshape(8, NC),
    )
    a, b, g = pl.pallas_call(
        publish,
        out_shape=(
            jax.ShapeDtypeStruct((4, NC), F32),
            jax.ShapeDtypeStruct((8, NC), F32),
            jax.ShapeDtypeStruct(pair, F32),
        ),
        in_specs=[pl.BlockSpec(memory_space=pl.ANY)] * 3,
        out_specs=(pl.BlockSpec(memory_space=pl.ANY),) * 3,
        scratch_shapes=[pltpu.SemaphoreType.DMA((3,))],
        name="publish",
    )(*(pltpu.with_memory_space_constraint(v, pltpu.VMEM) for v in (a, b, g)))
    return a.reshape(-1), b.reshape(-1), g


def solution(mesh, xn=4):
    dims = (mesh.shape["exp"] // (2 * xn), xn, mesh.shape["imp"])
    placed = (
        P(("exp", "imp"), None, None),
        P(("exp", "imp"), None, None),
        P(("exp", "imp")),
        P("exp"),
        P("imp"),
    )
    return jax.shard_map(
        functools.partial(per_device, dims),
        mesh=mesh,
        in_specs=placed,
        out_specs=(P("exp"), P("imp"), P()),
        check_vma=False,
    )
```

```python
import functools

import jax
import jax.numpy as jnp
from jax import lax
from jax.experimental import pallas as pl
from jax.experimental.pallas import tpu as pltpu
from jax.sharding import PartitionSpec as P

MESH = pl.DeviceIdType.MESH
RIDGE = 64.0
NC = 128
SIDE = 256
SLOTS = 4
F32 = jnp.float32
BF16 = jnp.bfloat16


def split(x):
    hi = x.astype(BF16)
    lo = (x - hi.astype(F32)).astype(BF16)
    return hi, lo


def dot(x, y):
    return lax.dot_general(x, y, (((1,), (0,)), ((), ())), preferred_element_type=F32)


def dot_nt(x, y):
    return lax.dot_general(x, y, (((1,), (1,)), ((), ())), preferred_element_type=F32)


def hops(off):
    return sum(min(o, 4 - o) for o in off[:3])


def order(offsets):
    return sorted((off for off in offsets if any(off)), key=hops, reverse=True)


def kernel(
    dims,
    routing_in,
    tile_block_in,
    flows,
    exp_ids_in,
    imp_ids_in,
    a_out,
    b_out,
    g_out,
    routing,
    tile_block,
    exp_ids,
    imp_ids,
    fbuf,
    row_t,
    row_s,
    col_t,
    col_s,
    x0,
    xq,
    mu,
    ubuf,
    wbuf,
    vbuf,
    va,
    vb,
    r0g,
    qg,
    eg,
    own,
    tabs,
    image,
    parts,
    gathered,
    zb,
    bb,
    hs,
    hb,
    ps,
    rsb,
    rxb,
    agb,
    fsem,
    z_sem,
    b_sem,
    h_sem,
    p_sem,
    rs_sem,
    rx_sem,
    ag_sem,
    part_sem,
    gath_sem,
):
    Y, XN, Z = dims
    E, XY = 2 * Y * XN, Y * XN
    chunk = NC // XY
    e = lax.axis_index("exp")
    m = lax.axis_index("imp")
    chip = lax.div(e, 2)
    core = lax.rem(e, 2)
    y = lax.div(chip, XN)
    x = lax.rem(chip, XN)
    zc = m * 2 + core

    def device(yy, xx, cc, mm):
        return ((yy * XN + xx) * 2 + cc, mm)

    def step_to(at, off, size):
        return lax.rem(at + off, size) if off else at

    z_dev = [(e, lax.rem(m + k, Z)) for k in range(1, Z)]
    xy_at = [
        (step_to(y, oy, Y), step_to(x, ox, XN)) for oy, ox in order([(i, k) for i in range(Y) for k in range(XN)])
    ]
    xy_dev = [device(yy, xx, core, m) for yy, xx in xy_at]

    def shift(oy, ox, oz, oc):
        return device(step_to(y, oy, Y), step_to(x, ox, XN), 1 - core if oc else core, step_to(m, oz, Z))

    ranges = [(i, k, q, c) for i in range(Y) for k in range(XN) for q in range(Z) for c in range(2)]
    far_dev = [shift(*off) for off in order(ranges) if hops(off) >= 5]
    mid_dev = [shift(*off) for off in order(ranges) if hops(off) == 4]
    near_dev = [shift(*off) for off in order(ranges) if hops(off) <= 3]
    all_dev = far_dev + mid_dev + near_dev
    me = e * Z + m
    own_rows = NC // (E * Z)
    plane_dev = [shift(*off) for off in order([off for off in ranges if off[2] == 0])]
    zc_dev = [
        device(y, x, 1 - core if oc else core, step_to(m, oz, Z))
        for oz, oc in order([(i, k) for i in range(Z) for k in range(2)])
    ]
    after, before = lax.rem(e + 1, E), lax.rem(e + E - 1, E)
    h_dev = [(after, lax.rem(m + k, Z)) for k in range(Z)], [(before, lax.rem(m + k, Z)) for k in range(Z)]
    xy = y * XN + x

    operands = (
        (tile_block_in, tile_block),
        (routing_in, routing),
        (exp_ids_in, exp_ids),
        (imp_ids_in, imp_ids),
        (flows, fbuf),
    )
    fetches = [pltpu.make_async_copy(src, dst, fsem.at[k]) for k, (src, dst) in enumerate(operands)]
    for fetch in fetches:
        fetch.start()

    barrier = pltpu.get_barrier_semaphore()
    greet = plane_dev + h_dev[0] + h_dev[1] + zc_dev
    for dev in greet:
        pl.semaphore_signal(barrier, inc=1, device_id=dev, device_id_type=MESH)

    for fetch in fetches[:4]:
        fetch.wait()

    def push(src, dst, sems, dev):
        pltpu.make_async_remote_copy(
            src_ref=src, dst_ref=dst, send_sem=sems.at[0], recv_sem=sems.at[1], device_id=dev, device_id_type=MESH
        ).start()

    def fan(src, sems, devs):
        for dev in devs:
            push(src, src, sems, dev)

    def arrive(whole, sems):
        for k in (1, 0):
            pltpu.make_async_copy(whole, whole, sems.at[k]).wait()

    riota = lax.broadcasted_iota(jnp.int32, (NC, NC), 0)
    ciota = lax.broadcasted_iota(jnp.int32, (NC, NC), 1)
    riota_f, ciota_f = riota.astype(F32), ciota.astype(F32)
    row_blk, col_blk, live = [], [], []
    for k in range(SLOTS):
        blk = tile_block[k]
        row_blk.append(lax.div(blk, 4))
        col_blk.append(lax.rem(blk, 4))
        hit = jnp.int32(0)
        for t in range(routing.shape[0]):
            hit = hit | jnp.where(routing[t] == k, 1, 0)
        live.append(hit)
    erow = [exp_ids[pl.ds(2 * row_blk[k] + h, 1), :] for k in range(SLOTS) for h in range(2)]
    irow = [imp_ids[pl.ds(2 * col_blk[k] + h, 1), :] for k in range(SLOTS) for h in range(2)]
    ids_t = jnp.concatenate(
        [v.astype(F32) for v in erow + irow] + [jnp.zeros((NC - 4 * SLOTS, NC), F32)], axis=0
    ).T
    for q in range(2 * SLOTS):
        k, h = divmod(q, 2)
        row_t[:, NC * q : NC * (q + 1)] = jnp.where(riota == erow[q], 1.0, 0.0).astype(BF16)
        row_s[NC * q : NC * (q + 1), :] = jnp.where(ciota_f == ids_t[:, q : q + 1], 1.0, 0.0).astype(BF16)
        hot = jnp.where(riota == irow[q], 1.0, 0.0).astype(BF16)
        col_t[k, 0:NC, NC * h : NC * (h + 1)] = hot
        col_t[k, NC : 2 * NC, NC * h : NC * (h + 1)] = hot
        col_s[NC * q : NC * (q + 1), :] = jnp.where(
            ciota_f == ids_t[:, 2 * SLOTS + q : 2 * SLOTS + q + 1], 1.0, 0.0
        ).astype(BF16)
    eids, iids = exp_ids[...].astype(F32), imp_ids[...].astype(F32)

    def least(v):
        return jnp.min(jnp.min(v, axis=0, keepdims=True), axis=1, keepdims=True)

    rf = jnp.broadcast_to(least(eids), (1, NC))
    rl = jnp.broadcast_to(-least(-eids), (1, NC))
    cf = jnp.broadcast_to(least(iids), (1, NC))
    cl = jnp.broadcast_to(-least(-iids), (1, NC))
    lane = lax.broadcasted_iota(jnp.int32, (1, NC), 1).astype(F32)
    zero_row = jnp.zeros((1, NC), F32)
    ends = jnp.concatenate(
        [jnp.where(lane == cf, 1.0, 0.0), jnp.where(lane == cl, 1.0, 0.0)] + [zero_row] * 6, axis=0
    ).astype(BF16)
    ones8 = jnp.ones((8, 2 * NC), BF16)
    row_w = [[jnp.where(row_blk[k] == c, 1.0, 0.0) for c in range(2)] for k in range(SLOTS)]
    col_w = [[jnp.where(col_blk[k] == c, 1.0, 0.0) for c in range(4)] for k in range(SLOTS)]

    def keep(k, v):
        return jnp.where(jnp.full(v.shape, live[k]) > 0, v, 0.0)

    def collect(cells):
        sums = []
        for k in range(SLOTS):
            w = cells(k)
            hi, lo = split(w)
            wbuf[k, :, 0:SIDE] = hi
            wbuf[k, :, SIDE : 2 * SIDE] = lo
            sums.append(jnp.sum(w, axis=0, keepdims=True))
        brows = []
        for c in range(4):
            for h in range(2):
                brows.append(sum(col_w[k][c] * sums[k][:, NC * h : NC * (h + 1)] for k in range(SLOTS)))
        return jnp.concatenate(brows, axis=0)

    def b_store(r, bpart):
        bb[r, e] = bpart

    def b_send(r):
        fan(bb.at[r, e], b_sem.at[r], plane_dev)

    def table_sums():
        for k in range(SLOTS):
            hot = col_s[SIDE * k : SIDE * (k + 1), :]
            vhi, vlo = split(dot(wbuf[k, :, 0:SIDE], hot) + dot(wbuf[k, :, SIDE : 2 * SIDE], hot))
            vbuf[SIDE * k : SIDE * (k + 1), 0:NC] = vhi
            vbuf[SIDE * k : SIDE * (k + 1), NC : 2 * NC] = vlo
        v = vbuf[...]
        wide = dot(row_t[...], v)
        table = wide[:, 0:NC] + wide[:, NC : 2 * NC]
        rsum = dot_nt(ones8, v)
        arows = []
        for c in range(2):
            for h in range(2):
                arows.append(
                    sum(
                        row_w[k][c] * rsum[0:1, SIDE * k + NC * h : SIDE * k + NC * (h + 1)]
                        for k in range(SLOTS)
                    )
                )
        return table, arows

    def table_store(r, table, arows):
        first = jnp.sum(jnp.where(riota_f == rf, table, 0.0), axis=0, keepdims=True)
        last = jnp.sum(jnp.where(riota_f == rl, table, 0.0), axis=0, keepdims=True)
        hs[r, 0] = jnp.concatenate([last, rl], axis=0)
        hs[r, 1] = jnp.concatenate([first, rf], axis=0)

    def rows_send(r):
        for side in range(2):
            for dev in h_dev[side]:
                push(hs.at[r, side], hb.at[r, side, m], h_sem.at[r], dev)

    def edge_store(r, table, arows):
        hi, lo = split(table)
        edge = dot_nt(ends, jnp.concatenate([hi, lo], axis=0))
        edge = edge[:, 0:NC] + edge[:, NC : 2 * NC]
        zb[r, m] = jnp.concatenate(arows + [edge[0:1], edge[1:2], cf, cl], axis=0)

    def edge_send(r):
        fan(zb.at[r, m], z_sem.at[r], z_dev)

    def table_send(r, table, arows):
        table_store(r, table, arows)
        rows_send(r)
        edge_store(r, table, arows)
        edge_send(r)

    def scal_store(s, rows):
        rows = jnp.sum(jnp.concatenate(rows + [zero_row] * (8 - len(rows)), axis=0), axis=1, keepdims=True)
        ps[s, pl.ds(me, 1), :] = sum(jnp.where(lane == float(k), rows[k : k + 1], 0.0) for k in range(3))

    def scal_fan(s, devs):
        fan(ps.at[s, pl.ds(me, 1)], p_sem.at[s], devs)

    def scal_total(s):
        arrive(ps.at[s, pl.ds(0, E * Z - 1)], p_sem.at[s])
        total = jnp.sum(ps[s], axis=0, keepdims=True)
        return [total[:, k : k + 1] for k in range(3)]

    def columns(r, avec):
        va[0:4, :] = avec
        tiles = [va[pl.ds(2 * row_blk[k] + h, 1), :] for k in range(SLOTS) for h in range(2)]
        prev = zb[r, lax.rem(m + Z - 1, Z), 5:6, :]
        nxt = zb[r, lax.rem(m + 1, Z), 4:5, :]
        return jnp.concatenate(tiles + [prev, nxt, jnp.zeros((NC - 10, NC), F32)], axis=0).T

    def table_end(r, table, cols):
        cl_prev = zb[r, lax.rem(m + Z - 1, Z), 7:8, :]
        cf_next = zb[r, lax.rem(m + 1, Z), 6:7, :]
        table = table + jnp.where(ciota_f == cl_prev, cols[:, 8:9], 0.0)
        table = table + jnp.where(ciota_f == cf_next, cols[:, 9:10], 0.0)
        arrive(hb.at[r], h_sem.at[r])
        from_prev, from_next = (sum(hb[r, side, k] for k in range(Z)) for side in range(2))
        rl_prev, rf_next = hb[r, 0, 0, 1:2, :], hb[r, 1, 0, 1:2, :]
        table = table + jnp.where(riota_f == rl_prev, from_prev[0:1], 0.0)
        table = table + jnp.where(riota_f == rf_next, from_next[0:1], 0.0)
        if r == 0:
            skip_r = jnp.where(rl_prev == rf, 1.0, 0.0)
            skip_c = jnp.where(cl_prev == cf, 1.0, 0.0)
            mine = (riota_f >= rf + skip_r) & (riota_f <= rl) & (ciota_f >= cf + skip_c) & (ciota_f <= cl)
            own[...] = jnp.where(mine, 1.0, 0.0)
        return table

    def z_end(r):
        arrive(zb.at[r, pl.ds(0, Z - 1)], z_sem.at[r])
        return sum(zb[r, k, 0:4, :] for k in range(Z))

    def b_end(r):
        arrive(bb.at[r, pl.ds(0, E - 1)], b_sem.at[r])
        return sum(bb[r, k] for k in range(E))

    def select(gval):
        hi, lo = split(gval)
        ubuf[...] = dot(row_s[...], jnp.concatenate([hi, lo], axis=1)).astype(BF16)

    def expand(cols, bvec):
        vb[...] = bvec

        def tile(k):
            brow = jnp.concatenate([vb[pl.ds(2 * col_blk[k] + h, 1), :] for h in range(2)], axis=1)
            acol = jnp.concatenate([cols[:, 2 * k + h : 2 * k + h + 1] for h in range(2)], axis=0)
            return dot(ubuf[SIDE * k : SIDE * (k + 1), :], col_t[k]) + acol + brow

        return tile

    def fold(v):
        v = jnp.sum(v.reshape(SIDE // 8, 8, SIDE), axis=0)
        return v[:, 0:NC] + v[:, NC:SIDE]

    def lanes(v):
        return jnp.sum(v, axis=0, keepdims=True)

    def inner(u, v):
        total = lanes(u[0] * v[0]) * (1.0 / Z) + lanes(u[1] * v[1]) * (1.0 / E)
        return total + lanes(own[...] * u[2] * v[2])

    def scatter():
        rsb[xy] = tabs[:, pl.ds(xy * chunk, chunk), :]
        for (yy, xx), dev in zip(xy_at, xy_dev):
            push(tabs.at[:, pl.ds((yy * XN + xx) * chunk, chunk)], rsb.at[xy], rs_sem, dev)

    def rows_out():
        parts[pl.ds(me * own_rows, own_rows), :] = image[pl.ds(me * own_rows, own_rows), :]
        for ee, mm in all_dev:
            src = image.at[pl.ds((ee * Z + mm) * own_rows, own_rows)]
            push(src, parts.at[pl.ds(me * own_rows, own_rows)], part_sem, (ee, mm))

    def rows_back():
        arrive(parts.at[pl.ds(0, NC - own_rows)], part_sem)
        gathered[pl.ds(me * own_rows, own_rows), :] = jnp.sum(
            parts[...].reshape(E * Z, own_rows, NC), axis=0
        ) if own_rows > 1 else jnp.sum(parts[...], axis=0, keepdims=True)
        fan(gathered.at[pl.ds(me * own_rows, own_rows)], gath_sem, all_dev)

    effects = None
    for newton in range(2):
        final = newton == 1
        r = 2 * newton
        if not final:

            def cells(k):
                mu[k] = keep(k, jnp.ones((SIDE, SIDE), F32))
                return keep(k, fbuf[k].astype(F32) - 1.0)

            fetches[4].wait()
        else:

            def cells(k):
                rate = keep(k, jnp.exp(c0 * x0[k] + c1 * (x0[k] - step * xq[k])))
                mu[k] = rate
                return keep(k, fbuf[k].astype(F32)) - rate

        bpart = collect(cells)
        b_store(r, bpart)
        if not final:
            table, arows = table_sums()
            table_store(r, table, arows)
            edge_store(r, table, arows)
            pl.semaphore_wait(barrier, len(greet))
            b_send(r)
            rows_send(r)
            edge_send(r)
        else:
            b_send(r)
            table, arows = table_sums()
            table_send(r, table, arows)
        if final:
            tabs[0] = eg[...] * own[...]
            tabs[1] = table
            scatter()
        ra = z_end(r)
        if final:
            ra = ra - RIDGE * effects[0]
        cols = columns(r, ra)
        rg = table_end(r, table, cols)
        if final:
            rg = rg - RIDGE * eg[...]
        r0g[...] = rg
        select(rg)
        rb = b_end(r)
        if final:
            rb = rb - RIDGE * effects[1]
        res = (ra, rb, rg)
        tile = expand(cols, rb)
        quad = []

        def cells(k):
            v = tile(k)
            x0[k] = v
            w = mu[k] * v
            quad.append(fold(w * v))
            return w

        bpart = collect(cells)
        scal_store(r, [inner(res, res), lanes(sum(quad))])
        scal_fan(r, far_dev)
        b_store(r + 1, bpart)
        b_send(r + 1)
        scal_fan(r, mid_dev)
        table, arows = table_sums()
        table_send(r + 1, table, arows)
        scal_fan(r, near_dev)
        if final:
            arrive(rsb.at[pl.ds(0, XY - 1)], rs_sem)
            rxb[zc] = sum(rsb[k] for k in range(XY))
            fan(rxb.at[zc], rx_sem, zc_dev)
            image[...] = table
            rows_out()
        qa = z_end(r + 1) + RIDGE * ra
        cols = columns(r + 1, qa)
        qgv = table_end(r + 1, table, cols) + RIDGE * r0g[...]
        qg[...] = qgv
        select(qgv)
        qb = b_end(r + 1) + RIDGE * rb
        tile = expand(cols, qb)
        for k in range(SLOTS):
            xq[k] = tile(k)
        rr, rhr, _ = scal_total(r)
        rhr = rhr + RIDGE * rr
        step = rr / rhr

        quad = []
        for k in range(SLOTS):
            v = x0[k] - step * xq[k]
            quad.append(fold(mu[k] * v * v))
        qvec = (qa, qb, qg[...])
        res1 = (ra - step * qa, rb - step * qb, r0g[...] - step * qg[...])
        scal_store(r + 1, [inner(res1, res1), lanes(sum(quad)), inner(res1, qvec)])
        scal_fan(r + 1, all_dev)
        if final:
            rows_back()
            arrive(rxb.at[pl.ds(0, 2 * Z - 1)], rx_sem)
            agb[xy] = sum(rxb[k] for k in range(2 * Z))
            fan(agb.at[xy], ag_sem, xy_dev)
        rr1, curve, cross = scal_total(r + 1)
        beta = rr1 / rr
        curve = curve + RIDGE * rr1 + 2.0 * beta * cross + beta * beta * rhr
        c1 = rr1 / curve
        c0 = step + c1 * beta
        da = c0 * ra + c1 * (ra - step * qa)
        db = c0 * rb + c1 * (rb - step * qb)
        if not final:
            effects = (da, db)
            eg[...] = c0 * r0g[...] + c1 * (r0g[...] - step * qg[...])
        else:
            a_out[...] = effects[0] + da
            b_out[...] = effects[1] + db
            arrive(agb.at[pl.ds(0, XY - 1)], ag_sem)
            arrive(gathered.at[pl.ds(0, NC - own_rows)], gath_sem)
            for k in range(XY):
                was = agb[k, 0]
                res0 = agb[k, 1] - RIDGE * was
                img = gathered[chunk * k : chunk * (k + 1), :] + RIDGE * res0
                g_out[chunk * k : chunk * (k + 1), :] = was + (c0 * res0 + c1 * (res0 - step * img))

def publish(a, b, g, a_out, b_out, g_out, sems):
    copies = [pltpu.make_async_copy(src, dst, sems.at[k]) for k, (src, dst) in enumerate(((g, g_out), (a, a_out), (b, b_out)))]
    for copy in copies:
        copy.start()
    for copy in copies:
        copy.wait()


def per_device(dims, flows, routing, tile_block, exp_country, imp_country):
    Y, XN, Z = dims
    XY = Y * XN
    chunk = NC // XY
    dma = pltpu.SemaphoreType.DMA
    vmem = functools.partial(pl.BlockSpec, memory_space=pltpu.VMEM)
    cells = SLOTS * SIDE
    pair = (NC, NC)
    sems = [dma((4, 2))] * 4 + [dma((2,))] * 5
    a, b, g = pl.pallas_call(
        functools.partial(kernel, dims),
        out_shape=(pltpu.VMEM((4, NC), F32), pltpu.VMEM((8, NC), F32), pltpu.VMEM(pair, F32)),
        in_specs=[pl.BlockSpec(memory_space=pl.ANY)] * 5,
        out_specs=(vmem(), vmem(), vmem()),
        scratch_shapes=[
            pltpu.SMEM((SLOTS,), jnp.int32),
            pltpu.SMEM((routing.size,), jnp.int32),
            pltpu.VMEM((4, NC), jnp.int32),
            pltpu.VMEM((8, NC), jnp.int32),
            pltpu.VMEM((SLOTS, SIDE, SIDE), BF16),
            pltpu.VMEM((NC, cells), BF16),
            pltpu.VMEM((cells, NC), BF16),
            pltpu.VMEM((SLOTS, 2 * NC, SIDE), BF16),
            pltpu.VMEM((cells, NC), BF16),
            pltpu.VMEM((SLOTS, SIDE, SIDE), F32),
            pltpu.VMEM((SLOTS, SIDE, SIDE), F32),
            pltpu.VMEM((SLOTS, SIDE, SIDE), F32),
            pltpu.VMEM((cells, 2 * NC), BF16),
            pltpu.VMEM((SLOTS, SIDE, 2 * SIDE), BF16),
            pltpu.VMEM((cells, 2 * NC), BF16),
            pltpu.VMEM((8, NC), F32),
            pltpu.VMEM((8, NC), F32),
            pltpu.VMEM(pair, F32),
            pltpu.VMEM(pair, F32),
            pltpu.VMEM(pair, F32),
            pltpu.VMEM(pair, F32),
            pltpu.VMEM((2,) + pair, F32),
            pltpu.VMEM(pair, F32),
            pltpu.VMEM(pair, F32),
            pltpu.VMEM(pair, F32),
            pltpu.VMEM((4, Z, 8, NC), F32),
            pltpu.VMEM((4, 2 * XY, 8, NC), F32),
            pltpu.VMEM((4, 2, 2, NC), F32),
            pltpu.VMEM((4, 2, Z, 2, NC), F32),
            pltpu.VMEM((4, 2 * XY * Z, NC), F32),
            pltpu.VMEM((XY, 2, chunk, NC), F32),
            pltpu.VMEM((2 * Z, 2, chunk, NC), F32),
            pltpu.VMEM((XY, 2, chunk, NC), F32),
            dma((5,)),
        ]
        + sems,
        compiler_params=pltpu.CompilerParams(collective_id=0, has_side_effects=True),
        name="gravity",
    )(
        routing.reshape(-1),
        tile_block,
        flows,
        exp_country.reshape(4, NC),
        imp_country.reshape(8, NC),
    )
    a, b, g = pl.pallas_call(
        publish,
        out_shape=(
            jax.ShapeDtypeStruct((4, NC), F32),
            jax.ShapeDtypeStruct((8, NC), F32),
            jax.ShapeDtypeStruct(pair, F32),
        ),
        in_specs=[pl.BlockSpec(memory_space=pl.ANY)] * 3,
        out_specs=(pl.BlockSpec(memory_space=pl.ANY),) * 3,
        scratch_shapes=[pltpu.SemaphoreType.DMA((3,))],
        name="publish",
    )(*(pltpu.with_memory_space_constraint(v, pltpu.VMEM) for v in (a, b, g)))
    return a.reshape(-1), b.reshape(-1), g


def solution(mesh, xn=4):
    dims = (mesh.shape["exp"] // (2 * xn), xn, mesh.shape["imp"])
    placed = (
        P(("exp", "imp"), None, None),
        P(("exp", "imp"), None, None),
        P(("exp", "imp")),
        P("exp"),
        P("imp"),
    )
    return jax.shard_map(
        functools.partial(per_device, dims),
        mesh=mesh,
        in_specs=placed,
        out_specs=(P("exp"), P("imp"), P()),
        check_vma=False,
    )
```

```python
import functools

import jax
import jax.numpy as jnp
from jax import lax
from jax.experimental import pallas as pl
from jax.experimental.pallas import tpu as pltpu
from jax.sharding import PartitionSpec as P

MESH = pl.DeviceIdType.MESH
RIDGE = 64.0
NC = 128
SIDE = 256
SLOTS = 4
F32 = jnp.float32
BF16 = jnp.bfloat16


def split(x):
    hi = x.astype(BF16)
    lo = (x - hi.astype(F32)).astype(BF16)
    return hi, lo


def dot(x, y):
    return lax.dot_general(x, y, (((1,), (0,)), ((), ())), preferred_element_type=F32)


def dot_nt(x, y):
    return lax.dot_general(x, y, (((1,), (1,)), ((), ())), preferred_element_type=F32)


def hops(off):
    return sum(min(o, 4 - o) for o in off[:3])


def order(offsets):
    return sorted((off for off in offsets if any(off)), key=hops, reverse=True)


def kernel(
    dims,
    routing_in,
    tile_block_in,
    flows,
    exp_ids_in,
    imp_ids_in,
    a_out,
    b_out,
    g_out,
    routing,
    tile_block,
    exp_ids,
    imp_ids,
    fbuf,
    row_t,
    row_s,
    col_t,
    col_s,
    x0,
    xq,
    mu,
    ubuf,
    wbuf,
    vbuf,
    va,
    vb,
    r0g,
    qg,
    eg,
    own,
    tabs,
    image,
    parts,
    gathered,
    zb,
    bb,
    hs,
    hb,
    ps,
    rsb,
    rxb,
    agb,
    fsem,
    z_sem,
    b_sem,
    h_sem,
    p_sem,
    rs_sem,
    rx_sem,
    ag_sem,
    part_sem,
    gath_sem,
):
    Y, XN, Z = dims
    E, XY = 2 * Y * XN, Y * XN
    chunk = NC // XY
    e = lax.axis_index("exp")
    m = lax.axis_index("imp")
    chip = lax.div(e, 2)
    core = lax.rem(e, 2)
    y = lax.div(chip, XN)
    x = lax.rem(chip, XN)
    zc = m * 2 + core

    def device(yy, xx, cc, mm):
        return ((yy * XN + xx) * 2 + cc, mm)

    def step_to(at, off, size):
        return lax.rem(at + off, size) if off else at

    z_dev = [(e, lax.rem(m + k, Z)) for k in range(1, Z)]
    xy_at = [
        (step_to(y, oy, Y), step_to(x, ox, XN)) for oy, ox in order([(i, k) for i in range(Y) for k in range(XN)])
    ]
    xy_dev = [device(yy, xx, core, m) for yy, xx in xy_at]

    def shift(oy, ox, oz, oc):
        return device(step_to(y, oy, Y), step_to(x, ox, XN), 1 - core if oc else core, step_to(m, oz, Z))

    ranges = [(i, k, q, c) for i in range(Y) for k in range(XN) for q in range(Z) for c in range(2)]
    far_dev = [shift(*off) for off in order(ranges) if hops(off) >= 5]
    mid_dev = [shift(*off) for off in order(ranges) if hops(off) == 4]
    near_dev = [shift(*off) for off in order(ranges) if hops(off) <= 3]
    all_dev = far_dev + mid_dev + near_dev
    me = e * Z + m
    own_rows = NC // (E * Z)
    plane_dev = [shift(*off) for off in order([off for off in ranges if off[2] == 0])]
    zc_dev = [
        device(y, x, 1 - core if oc else core, step_to(m, oz, Z))
        for oz, oc in order([(i, k) for i in range(Z) for k in range(2)])
    ]
    after, before = lax.rem(e + 1, E), lax.rem(e + E - 1, E)
    h_dev = [(after, lax.rem(m + k, Z)) for k in range(Z)], [(before, lax.rem(m + k, Z)) for k in range(Z)]
    xy = y * XN + x

    operands = (
        (tile_block_in, tile_block),
        (routing_in, routing),
        (exp_ids_in, exp_ids),
        (imp_ids_in, imp_ids),
        (flows, fbuf),
    )
    fetches = [pltpu.make_async_copy(src, dst, fsem.at[k]) for k, (src, dst) in enumerate(operands)]
    for fetch in fetches:
        fetch.start()

    barrier = pltpu.get_barrier_semaphore()
    greet = plane_dev + h_dev[0] + h_dev[1] + zc_dev
    for dev in greet:
        pl.semaphore_signal(barrier, inc=1, device_id=dev, device_id_type=MESH)

    for fetch in fetches[:4]:
        fetch.wait()

    def push(src, dst, sems, dev):
        pltpu.make_async_remote_copy(
            src_ref=src, dst_ref=dst, send_sem=sems.at[0], recv_sem=sems.at[1], device_id=dev, device_id_type=MESH
        ).start()

    def fan(src, sems, devs):
        for dev in devs:
            push(src, src, sems, dev)

    def arrive(whole, sems):
        for k in (1, 0):
            pltpu.make_async_copy(whole, whole, sems.at[k]).wait()

    riota = lax.broadcasted_iota(jnp.int32, (NC, NC), 0)
    ciota = lax.broadcasted_iota(jnp.int32, (NC, NC), 1)
    riota_f, ciota_f = riota.astype(F32), ciota.astype(F32)
    row_blk, col_blk, live = [], [], []
    for k in range(SLOTS):
        blk = tile_block[k]
        row_blk.append(lax.div(blk, 4))
        col_blk.append(lax.rem(blk, 4))
        hit = jnp.int32(0)
        for t in range(routing.shape[0]):
            hit = hit | jnp.where(routing[t] == k, 1, 0)
        live.append(hit)
    erow = [exp_ids[pl.ds(2 * row_blk[k] + h, 1), :] for k in range(SLOTS) for h in range(2)]
    irow = [imp_ids[pl.ds(2 * col_blk[k] + h, 1), :] for k in range(SLOTS) for h in range(2)]
    ids_t = jnp.concatenate(
        [v.astype(F32) for v in erow + irow] + [jnp.zeros((NC - 4 * SLOTS, NC), F32)], axis=0
    ).T
    for q in range(2 * SLOTS):
        k, h = divmod(q, 2)
        row_t[:, NC * q : NC * (q + 1)] = jnp.where(riota == erow[q], 1.0, 0.0).astype(BF16)
        row_s[NC * q : NC * (q + 1), :] = jnp.where(ciota_f == ids_t[:, q : q + 1], 1.0, 0.0).astype(BF16)
        hot = jnp.where(riota == irow[q], 1.0, 0.0).astype(BF16)
        col_t[k, 0:NC, NC * h : NC * (h + 1)] = hot
        col_t[k, NC : 2 * NC, NC * h : NC * (h + 1)] = hot
        col_s[NC * q : NC * (q + 1), :] = jnp.where(
            ciota_f == ids_t[:, 2 * SLOTS + q : 2 * SLOTS + q + 1], 1.0, 0.0
        ).astype(BF16)
    eids, iids = exp_ids[...].astype(F32), imp_ids[...].astype(F32)

    def least(v):
        return jnp.min(jnp.min(v, axis=0, keepdims=True), axis=1, keepdims=True)

    rf = jnp.broadcast_to(least(eids), (1, NC))
    rl = jnp.broadcast_to(-least(-eids), (1, NC))
    cf = jnp.broadcast_to(least(iids), (1, NC))
    cl = jnp.broadcast_to(-least(-iids), (1, NC))
    lane = lax.broadcasted_iota(jnp.int32, (1, NC), 1).astype(F32)
    zero_row = jnp.zeros((1, NC), F32)
    ends = jnp.concatenate(
        [jnp.where(lane == cf, 1.0, 0.0), jnp.where(lane == cl, 1.0, 0.0)] + [zero_row] * 6, axis=0
    ).astype(BF16)
    ones8 = jnp.ones((8, 2 * NC), BF16)
    row_w = [[jnp.where(row_blk[k] == c, 1.0, 0.0) for c in range(2)] for k in range(SLOTS)]
    col_w = [[jnp.where(col_blk[k] == c, 1.0, 0.0) for c in range(4)] for k in range(SLOTS)]

    def keep(k, v):
        return jnp.where(jnp.full(v.shape, live[k]) > 0, v, 0.0)

    def collect(cells):
        sums = []
        for k in range(SLOTS):
            w = cells(k)
            hi, lo = split(w)
            wbuf[k, :, 0:SIDE] = hi
            wbuf[k, :, SIDE : 2 * SIDE] = lo
            sums.append(jnp.sum(w, axis=0, keepdims=True))
        brows = []
        for c in range(4):
            for h in range(2):
                brows.append(sum(col_w[k][c] * sums[k][:, NC * h : NC * (h + 1)] for k in range(SLOTS)))
        return jnp.concatenate(brows, axis=0)

    def b_store(r, bpart):
        bb[r, e] = bpart

    def b_send(r):
        fan(bb.at[r, e], b_sem.at[r], plane_dev)

    def table_sums():
        for k in range(SLOTS):
            hot = col_s[SIDE * k : SIDE * (k + 1), :]
            vhi, vlo = split(dot(wbuf[k, :, 0:SIDE], hot) + dot(wbuf[k, :, SIDE : 2 * SIDE], hot))
            vbuf[SIDE * k : SIDE * (k + 1), 0:NC] = vhi
            vbuf[SIDE * k : SIDE * (k + 1), NC : 2 * NC] = vlo
        v = vbuf[...]
        wide = dot(row_t[...], v)
        table = wide[:, 0:NC] + wide[:, NC : 2 * NC]
        rsum = dot_nt(ones8, v)
        arows = []
        for c in range(2):
            for h in range(2):
                arows.append(
                    sum(
                        row_w[k][c] * rsum[0:1, SIDE * k + NC * h : SIDE * k + NC * (h + 1)]
                        for k in range(SLOTS)
                    )
                )
        return table, arows

    def table_store(r, table, arows):
        first = jnp.sum(jnp.where(riota_f == rf, table, 0.0), axis=0, keepdims=True)
        last = jnp.sum(jnp.where(riota_f == rl, table, 0.0), axis=0, keepdims=True)
        hs[r, 0] = jnp.concatenate([last, rl], axis=0)
        hs[r, 1] = jnp.concatenate([first, rf], axis=0)

    def rows_send(r):
        for side in range(2):
            for dev in h_dev[side]:
                push(hs.at[r, side], hb.at[r, side, m], h_sem.at[r], dev)

    def edge_store(r, table, arows):
        hi, lo = split(table)
        edge = dot_nt(ends, jnp.concatenate([hi, lo], axis=0))
        edge = edge[:, 0:NC] + edge[:, NC : 2 * NC]
        zb[r, m] = jnp.concatenate(arows + [edge[0:1], edge[1:2], cf, cl], axis=0)

    def edge_send(r):
        fan(zb.at[r, m], z_sem.at[r], z_dev)

    def table_send(r, table, arows):
        table_store(r, table, arows)
        rows_send(r)
        edge_store(r, table, arows)
        edge_send(r)

    def scal_store(s, rows):
        rows = jnp.sum(jnp.concatenate(rows + [zero_row] * (8 - len(rows)), axis=0), axis=1, keepdims=True)
        ps[s, pl.ds(me, 1), :] = sum(jnp.where(lane == float(k), rows[k : k + 1], 0.0) for k in range(3))

    def scal_fan(s, devs):
        fan(ps.at[s, pl.ds(me, 1)], p_sem.at[s], devs)

    def scal_total(s):
        arrive(ps.at[s, pl.ds(0, E * Z - 1)], p_sem.at[s])
        total = jnp.sum(ps[s], axis=0, keepdims=True)
        return [total[:, k : k + 1] for k in range(3)]

    def columns(r, avec):
        va[0:4, :] = avec
        tiles = [va[pl.ds(2 * row_blk[k] + h, 1), :] for k in range(SLOTS) for h in range(2)]
        prev = zb[r, lax.rem(m + Z - 1, Z), 5:6, :]
        nxt = zb[r, lax.rem(m + 1, Z), 4:5, :]
        return jnp.concatenate(tiles + [prev, nxt, jnp.zeros((NC - 10, NC), F32)], axis=0).T

    def table_end(r, table, cols):
        cl_prev = zb[r, lax.rem(m + Z - 1, Z), 7:8, :]
        cf_next = zb[r, lax.rem(m + 1, Z), 6:7, :]
        table = table + jnp.where(ciota_f == cl_prev, cols[:, 8:9], 0.0)
        table = table + jnp.where(ciota_f == cf_next, cols[:, 9:10], 0.0)
        arrive(hb.at[r], h_sem.at[r])
        from_prev, from_next = (sum(hb[r, side, k] for k in range(Z)) for side in range(2))
        rl_prev, rf_next = hb[r, 0, 0, 1:2, :], hb[r, 1, 0, 1:2, :]
        table = table + jnp.where(riota_f == rl_prev, from_prev[0:1], 0.0)
        table = table + jnp.where(riota_f == rf_next, from_next[0:1], 0.0)
        if r == 0:
            skip_r = jnp.where(rl_prev == rf, 1.0, 0.0)
            skip_c = jnp.where(cl_prev == cf, 1.0, 0.0)
            mine = (riota_f >= rf + skip_r) & (riota_f <= rl) & (ciota_f >= cf + skip_c) & (ciota_f <= cl)
            own[...] = jnp.where(mine, 1.0, 0.0)
        return table

    def z_end(r):
        arrive(zb.at[r, pl.ds(0, Z - 1)], z_sem.at[r])
        return sum(zb[r, k, 0:4, :] for k in range(Z))

    def b_end(r):
        arrive(bb.at[r, pl.ds(0, E - 1)], b_sem.at[r])
        return sum(bb[r, k] for k in range(E))

    def select(gval):
        hi, lo = split(gval)
        ubuf[...] = dot(row_s[...], jnp.concatenate([hi, lo], axis=1)).astype(BF16)

    def expand(cols, bvec):
        vb[...] = bvec

        def tile(k):
            brow = jnp.concatenate([vb[pl.ds(2 * col_blk[k] + h, 1), :] for h in range(2)], axis=1)
            acol = jnp.concatenate([cols[:, 2 * k + h : 2 * k + h + 1] for h in range(2)], axis=0)
            return dot(ubuf[SIDE * k : SIDE * (k + 1), :], col_t[k]) + acol + brow

        return tile

    def fold(v):
        v = jnp.sum(v.reshape(SIDE // 8, 8, SIDE), axis=0)
        return v[:, 0:NC] + v[:, NC:SIDE]

    def lanes(v):
        return jnp.sum(v, axis=0, keepdims=True)

    def inner(u, v):
        total = lanes(u[0] * v[0]) * (1.0 / Z) + lanes(u[1] * v[1]) * (1.0 / E)
        return total + lanes(own[...] * u[2] * v[2])

    def scatter():
        rsb[xy] = tabs[:, pl.ds(xy * chunk, chunk), :]
        for (yy, xx), dev in zip(xy_at, xy_dev):
            push(tabs.at[:, pl.ds((yy * XN + xx) * chunk, chunk)], rsb.at[xy], rs_sem, dev)

    def rows_out():
        parts[pl.ds(me * own_rows, own_rows), :] = image[pl.ds(me * own_rows, own_rows), :]
        for ee, mm in all_dev:
            src = image.at[pl.ds((ee * Z + mm) * own_rows, own_rows)]
            push(src, parts.at[pl.ds(me * own_rows, own_rows)], part_sem, (ee, mm))

    def rows_back():
        arrive(parts.at[pl.ds(0, NC - own_rows)], part_sem)
        gathered[pl.ds(me * own_rows, own_rows), :] = jnp.sum(
            parts[...].reshape(E * Z, own_rows, NC), axis=0
        ) if own_rows > 1 else jnp.sum(parts[...], axis=0, keepdims=True)
        fan(gathered.at[pl.ds(me * own_rows, own_rows)], gath_sem, all_dev)

    effects = None
    for newton in range(2):
        final = newton == 1
        r = 2 * newton
        if not final:

            def cells(k):
                mu[k] = keep(k, jnp.ones((SIDE, SIDE), F32))
                return keep(k, fbuf[k].astype(F32) - 1.0)

            fetches[4].wait()
        else:

            def cells(k):
                rate = keep(k, jnp.exp(both * x0[k] - shrink * xq[k]))
                mu[k] = rate
                return keep(k, fbuf[k].astype(F32)) - rate

        bpart = collect(cells)
        b_store(r, bpart)
        if not final:
            table, arows = table_sums()
            table_store(r, table, arows)
            edge_store(r, table, arows)
            pl.semaphore_wait(barrier, len(greet))
            rows_send(r)
            b_send(r)
            edge_send(r)
        else:
            b_send(r)
            table, arows = table_sums()
            table_send(r, table, arows)
        if final:
            tabs[0] = eg[...] * own[...]
            tabs[1] = table
            scatter()
        ra = z_end(r)
        if final:
            ra = ra - RIDGE * effects[0]
        cols = columns(r, ra)
        rg = table_end(r, table, cols)
        if final:
            rg = rg - RIDGE * eg[...]
        r0g[...] = rg
        select(rg)
        rb = b_end(r)
        if final:
            rb = rb - RIDGE * effects[1]
        res = (ra, rb, rg)
        tile = expand(cols, rb)
        quad = []

        def cells(k):
            v = tile(k)
            x0[k] = v
            w = mu[k] * v
            quad.append(fold(w * v))
            return w

        bpart = collect(cells)
        scal_store(r, [inner(res, res), lanes(sum(quad))])
        scal_fan(r, far_dev)
        b_store(r + 1, bpart)
        b_send(r + 1)
        table, arows = table_sums()
        table_store(r + 1, table, arows)
        rows_send(r + 1)
        scal_fan(r, mid_dev)
        edge_store(r + 1, table, arows)
        edge_send(r + 1)
        scal_fan(r, near_dev)
        if final:
            arrive(rsb.at[pl.ds(0, XY - 1)], rs_sem)
            rxb[zc] = sum(rsb[k] for k in range(XY))
            fan(rxb.at[zc], rx_sem, zc_dev)
            image[...] = table
            rows_out()
        qa = z_end(r + 1) + RIDGE * ra
        cols = columns(r + 1, qa)
        qgv = table_end(r + 1, table, cols) + RIDGE * r0g[...]
        qg[...] = qgv
        select(qgv)
        qb = b_end(r + 1) + RIDGE * rb
        tile = expand(cols, qb)
        for k in range(SLOTS):
            xq[k] = tile(k)
        rr, rhr, _ = scal_total(r)
        rhr = rhr + RIDGE * rr
        step = rr / rhr

        quad = []
        for k in range(SLOTS):
            v = x0[k] - step * xq[k]
            quad.append(fold(mu[k] * (v * v)))
        qvec = (qa, qb, qg[...])
        res1 = (ra - step * qa, rb - step * qb, r0g[...] - step * qg[...])
        scal_store(r + 1, [inner(res1, res1), lanes(sum(quad)), inner(res1, qvec)])
        scal_fan(r + 1, all_dev)
        if final:
            rows_back()
            arrive(rxb.at[pl.ds(0, 2 * Z - 1)], rx_sem)
            agb[xy] = sum(rxb[k] for k in range(2 * Z))
            fan(agb.at[xy], ag_sem, xy_dev)
        rr1, curve, cross = scal_total(r + 1)
        beta = rr1 / rr
        curve = curve + RIDGE * rr1 + 2.0 * beta * cross + beta * beta * rhr
        c1 = rr1 / curve
        c0 = step + c1 * beta
        both, shrink = c0 + c1, c1 * step
        da = c0 * ra + c1 * (ra - step * qa)
        db = c0 * rb + c1 * (rb - step * qb)
        if not final:
            effects = (da, db)
            eg[...] = c0 * r0g[...] + c1 * (r0g[...] - step * qg[...])
        else:
            a_out[...] = effects[0] + da
            b_out[...] = effects[1] + db
            arrive(agb.at[pl.ds(0, XY - 1)], ag_sem)
            arrive(gathered.at[pl.ds(0, NC - own_rows)], gath_sem)
            for k in range(XY):
                was = agb[k, 0]
                res0 = agb[k, 1] - RIDGE * was
                img = gathered[chunk * k : chunk * (k + 1), :] + RIDGE * res0
                g_out[chunk * k : chunk * (k + 1), :] = was + (c0 * res0 + c1 * (res0 - step * img))

def publish(a, b, g, a_out, b_out, g_out, sems):
    copies = [pltpu.make_async_copy(src, dst, sems.at[k]) for k, (src, dst) in enumerate(((g, g_out), (a, a_out), (b, b_out)))]
    for copy in copies:
        copy.start()
    for copy in copies:
        copy.wait()


def per_device(dims, flows, routing, tile_block, exp_country, imp_country):
    Y, XN, Z = dims
    XY = Y * XN
    chunk = NC // XY
    dma = pltpu.SemaphoreType.DMA
    vmem = functools.partial(pl.BlockSpec, memory_space=pltpu.VMEM)
    cells = SLOTS * SIDE
    pair = (NC, NC)
    sems = [dma((4, 2))] * 4 + [dma((2,))] * 5
    a, b, g = pl.pallas_call(
        functools.partial(kernel, dims),
        out_shape=(pltpu.VMEM((4, NC), F32), pltpu.VMEM((8, NC), F32), pltpu.VMEM(pair, F32)),
        in_specs=[pl.BlockSpec(memory_space=pl.ANY)] * 5,
        out_specs=(vmem(), vmem(), vmem()),
        scratch_shapes=[
            pltpu.SMEM((SLOTS,), jnp.int32),
            pltpu.SMEM((routing.size,), jnp.int32),
            pltpu.VMEM((4, NC), jnp.int32),
            pltpu.VMEM((8, NC), jnp.int32),
            pltpu.VMEM((SLOTS, SIDE, SIDE), BF16),
            pltpu.VMEM((NC, cells), BF16),
            pltpu.VMEM((cells, NC), BF16),
            pltpu.VMEM((SLOTS, 2 * NC, SIDE), BF16),
            pltpu.VMEM((cells, NC), BF16),
            pltpu.VMEM((SLOTS, SIDE, SIDE), F32),
            pltpu.VMEM((SLOTS, SIDE, SIDE), F32),
            pltpu.VMEM((SLOTS, SIDE, SIDE), F32),
            pltpu.VMEM((cells, 2 * NC), BF16),
            pltpu.VMEM((SLOTS, SIDE, 2 * SIDE), BF16),
            pltpu.VMEM((cells, 2 * NC), BF16),
            pltpu.VMEM((8, NC), F32),
            pltpu.VMEM((8, NC), F32),
            pltpu.VMEM(pair, F32),
            pltpu.VMEM(pair, F32),
            pltpu.VMEM(pair, F32),
            pltpu.VMEM(pair, F32),
            pltpu.VMEM((2,) + pair, F32),
            pltpu.VMEM(pair, F32),
            pltpu.VMEM(pair, F32),
            pltpu.VMEM(pair, F32),
            pltpu.VMEM((4, Z, 8, NC), F32),
            pltpu.VMEM((4, 2 * XY, 8, NC), F32),
            pltpu.VMEM((4, 2, 2, NC), F32),
            pltpu.VMEM((4, 2, Z, 2, NC), F32),
            pltpu.VMEM((4, 2 * XY * Z, NC), F32),
            pltpu.VMEM((XY, 2, chunk, NC), F32),
            pltpu.VMEM((2 * Z, 2, chunk, NC), F32),
            pltpu.VMEM((XY, 2, chunk, NC), F32),
            dma((5,)),
        ]
        + sems,
        compiler_params=pltpu.CompilerParams(collective_id=0, has_side_effects=True),
        name="gravity",
    )(
        routing.reshape(-1),
        tile_block,
        flows,
        exp_country.reshape(4, NC),
        imp_country.reshape(8, NC),
    )
    a, b, g = pl.pallas_call(
        publish,
        out_shape=(
            jax.ShapeDtypeStruct((4, NC), F32),
            jax.ShapeDtypeStruct((8, NC), F32),
            jax.ShapeDtypeStruct(pair, F32),
        ),
        in_specs=[pl.BlockSpec(memory_space=pl.ANY)] * 3,
        out_specs=(pl.BlockSpec(memory_space=pl.ANY),) * 3,
        scratch_shapes=[pltpu.SemaphoreType.DMA((3,))],
        name="publish",
    )(*(pltpu.with_memory_space_constraint(v, pltpu.VMEM) for v in (a, b, g)))
    return a.reshape(-1), b.reshape(-1), g


def solution(mesh, xn=4):
    dims = (mesh.shape["exp"] // (2 * xn), xn, mesh.shape["imp"])
    placed = (
        P(("exp", "imp"), None, None),
        P(("exp", "imp"), None, None),
        P(("exp", "imp")),
        P("exp"),
        P("imp"),
    )
    return jax.shard_map(
        functools.partial(per_device, dims),
        mesh=mesh,
        in_specs=placed,
        out_specs=(P("exp"), P("imp"), P()),
        check_vma=False,
    )
```

```python
import functools

import jax
import jax.numpy as jnp
from jax import lax
from jax.experimental import pallas as pl
from jax.experimental.pallas import tpu as pltpu
from jax.sharding import PartitionSpec as P

MESH = pl.DeviceIdType.MESH
RIDGE = 64.0
NC = 128
SIDE = 256
SLOTS = 4
F32 = jnp.float32
BF16 = jnp.bfloat16


def split(x):
    hi = x.astype(BF16)
    lo = (x - hi.astype(F32)).astype(BF16)
    return hi, lo


def dot(x, y):
    return lax.dot_general(x, y, (((1,), (0,)), ((), ())), preferred_element_type=F32)


def dot_nt(x, y):
    return lax.dot_general(x, y, (((1,), (1,)), ((), ())), preferred_element_type=F32)


def hops(off):
    return sum(min(o, 4 - o) for o in off[:3])


def order(offsets):
    return sorted((off for off in offsets if any(off)), key=hops, reverse=True)


def kernel(
    dims,
    routing_in,
    tile_block_in,
    flows,
    exp_ids_in,
    imp_ids_in,
    a_out,
    b_out,
    g_out,
    routing,
    tile_block,
    exp_ids,
    imp_ids,
    fbuf,
    row_t,
    row_s,
    col_t,
    col_s,
    x0,
    xq,
    mu,
    ubuf,
    wbuf,
    vbuf,
    va,
    vb,
    r0g,
    qg,
    eg,
    own,
    tabs,
    image,
    parts,
    gathered,
    zb,
    bb,
    hs,
    hb,
    ps,
    rsb,
    rxb,
    agb,
    fsem,
    z_sem,
    b_sem,
    h_sem,
    p_sem,
    rs_sem,
    rx_sem,
    ag_sem,
    part_sem,
    gath_sem,
):
    Y, XN, Z = dims
    E, XY = 2 * Y * XN, Y * XN
    chunk = NC // XY
    e = lax.axis_index("exp")
    m = lax.axis_index("imp")
    chip = lax.div(e, 2)
    core = lax.rem(e, 2)
    y = lax.div(chip, XN)
    x = lax.rem(chip, XN)
    zc = m * 2 + core

    def device(yy, xx, cc, mm):
        return ((yy * XN + xx) * 2 + cc, mm)

    def step_to(at, off, size):
        return lax.rem(at + off, size) if off else at

    z_dev = [(e, lax.rem(m + k, Z)) for k in range(1, Z)]
    xy_at = [
        (step_to(y, oy, Y), step_to(x, ox, XN)) for oy, ox in order([(i, k) for i in range(Y) for k in range(XN)])
    ]
    xy_dev = [device(yy, xx, core, m) for yy, xx in xy_at]

    def shift(oy, ox, oz, oc):
        return device(step_to(y, oy, Y), step_to(x, ox, XN), 1 - core if oc else core, step_to(m, oz, Z))

    ranges = [(i, k, q, c) for i in range(Y) for k in range(XN) for q in range(Z) for c in range(2)]
    far_dev = [shift(*off) for off in order(ranges) if hops(off) >= 5]
    mid_dev = [shift(*off) for off in order(ranges) if hops(off) == 4]
    near_dev = [shift(*off) for off in order(ranges) if hops(off) <= 3]
    all_dev = far_dev + mid_dev + near_dev
    me = e * Z + m
    own_rows = NC // (E * Z)
    plane_dev = [shift(*off) for off in order([off for off in ranges if off[2] == 0])]
    zc_dev = [
        device(y, x, 1 - core if oc else core, step_to(m, oz, Z))
        for oz, oc in order([(i, k) for i in range(Z) for k in range(2)])
    ]
    after, before = lax.rem(e + 1, E), lax.rem(e + E - 1, E)
    h_dev = [(after, lax.rem(m + k, Z)) for k in range(Z)], [(before, lax.rem(m + k, Z)) for k in range(Z)]
    xy = y * XN + x

    operands = (
        (tile_block_in, tile_block),
        (routing_in, routing),
        (exp_ids_in, exp_ids),
        (imp_ids_in, imp_ids),
        (flows, fbuf),
    )
    fetches = [pltpu.make_async_copy(src, dst, fsem.at[k]) for k, (src, dst) in enumerate(operands)]
    for fetch in fetches:
        fetch.start()

    barrier = pltpu.get_barrier_semaphore()
    greet = plane_dev + h_dev[0] + h_dev[1] + zc_dev
    for dev in greet:
        pl.semaphore_signal(barrier, inc=1, device_id=dev, device_id_type=MESH)

    for fetch in fetches[:4]:
        fetch.wait()

    def push(src, dst, sems, dev):
        pltpu.make_async_remote_copy(
            src_ref=src, dst_ref=dst, send_sem=sems.at[0], recv_sem=sems.at[1], device_id=dev, device_id_type=MESH
        ).start()

    def fan(src, sems, devs):
        for dev in devs:
            push(src, src, sems, dev)

    def arrive(whole, sems):
        for k in (1, 0):
            pltpu.make_async_copy(whole, whole, sems.at[k]).wait()

    riota = lax.broadcasted_iota(jnp.int32, (NC, NC), 0)
    ciota = lax.broadcasted_iota(jnp.int32, (NC, NC), 1)
    riota_f, ciota_f = riota.astype(F32), ciota.astype(F32)
    row_blk, col_blk, live = [], [], []
    for k in range(SLOTS):
        blk = tile_block[k]
        row_blk.append(lax.div(blk, 4))
        col_blk.append(lax.rem(blk, 4))
        hit = jnp.int32(0)
        for t in range(routing.shape[0]):
            hit = hit | jnp.where(routing[t] == k, 1, 0)
        live.append(hit)
    erow = [exp_ids[pl.ds(2 * row_blk[k] + h, 1), :] for k in range(SLOTS) for h in range(2)]
    irow = [imp_ids[pl.ds(2 * col_blk[k] + h, 1), :] for k in range(SLOTS) for h in range(2)]
    ids_t = jnp.concatenate(
        [v.astype(F32) for v in erow + irow] + [jnp.zeros((NC - 4 * SLOTS, NC), F32)], axis=0
    ).T
    for q in range(2 * SLOTS):
        k, h = divmod(q, 2)
        row_t[:, NC * q : NC * (q + 1)] = jnp.where(riota == erow[q], 1.0, 0.0).astype(BF16)
        row_s[NC * q : NC * (q + 1), :] = jnp.where(ciota_f == ids_t[:, q : q + 1], 1.0, 0.0).astype(BF16)
        hot = jnp.where(riota == irow[q], 1.0, 0.0).astype(BF16)
        col_t[k, 0:NC, NC * h : NC * (h + 1)] = hot
        col_t[k, NC : 2 * NC, NC * h : NC * (h + 1)] = hot
        col_s[NC * q : NC * (q + 1), :] = jnp.where(
            ciota_f == ids_t[:, 2 * SLOTS + q : 2 * SLOTS + q + 1], 1.0, 0.0
        ).astype(BF16)
    eids, iids = exp_ids[...].astype(F32), imp_ids[...].astype(F32)

    def least(v):
        return jnp.min(jnp.min(v, axis=0, keepdims=True), axis=1, keepdims=True)

    rf = jnp.broadcast_to(least(eids), (1, NC))
    rl = jnp.broadcast_to(-least(-eids), (1, NC))
    cf = jnp.broadcast_to(least(iids), (1, NC))
    cl = jnp.broadcast_to(-least(-iids), (1, NC))
    lane = lax.broadcasted_iota(jnp.int32, (1, NC), 1).astype(F32)
    zero_row = jnp.zeros((1, NC), F32)
    ends = jnp.concatenate(
        [jnp.where(lane == cf, 1.0, 0.0), jnp.where(lane == cl, 1.0, 0.0)] + [zero_row] * 6, axis=0
    ).astype(BF16)
    ones8 = jnp.ones((8, 2 * NC), BF16)
    row_w = [[jnp.where(row_blk[k] == c, 1.0, 0.0) for c in range(2)] for k in range(SLOTS)]
    col_w = [[jnp.where(col_blk[k] == c, 1.0, 0.0) for c in range(4)] for k in range(SLOTS)]

    def keep(k, v):
        return jnp.where(jnp.full(v.shape, live[k]) > 0, v, 0.0)

    def collect(cells):
        sums = []
        for k in range(SLOTS):
            w = cells(k)
            hi, lo = split(w)
            wbuf[k, :, 0:SIDE] = hi
            wbuf[k, :, SIDE : 2 * SIDE] = lo
            sums.append(jnp.sum(w, axis=0, keepdims=True))
        brows = []
        for c in range(4):
            for h in range(2):
                brows.append(sum(col_w[k][c] * sums[k][:, NC * h : NC * (h + 1)] for k in range(SLOTS)))
        return jnp.concatenate(brows, axis=0)

    def b_store(r, bpart):
        bb[r, e] = bpart

    def b_send(r):
        fan(bb.at[r, e], b_sem.at[r], plane_dev)

    def table_sums():
        for k in range(SLOTS):
            hot = col_s[SIDE * k : SIDE * (k + 1), :]
            vhi, vlo = split(dot(wbuf[k, :, 0:SIDE], hot) + dot(wbuf[k, :, SIDE : 2 * SIDE], hot))
            vbuf[SIDE * k : SIDE * (k + 1), 0:NC] = vhi
            vbuf[SIDE * k : SIDE * (k + 1), NC : 2 * NC] = vlo
        v = vbuf[...]
        wide = dot(row_t[...], v)
        table = wide[:, 0:NC] + wide[:, NC : 2 * NC]
        rsum = dot_nt(ones8, v)
        arows = []
        for c in range(2):
            for h in range(2):
                arows.append(
                    sum(
                        row_w[k][c] * rsum[0:1, SIDE * k + NC * h : SIDE * k + NC * (h + 1)]
                        for k in range(SLOTS)
                    )
                )
        return table, arows

    def table_store(r, table, arows):
        first = jnp.sum(jnp.where(riota_f == rf, table, 0.0), axis=0, keepdims=True)
        last = jnp.sum(jnp.where(riota_f == rl, table, 0.0), axis=0, keepdims=True)
        hs[r, 0] = jnp.concatenate([last, rl], axis=0)
        hs[r, 1] = jnp.concatenate([first, rf], axis=0)

    def rows_send(r):
        for side in range(2):
            for dev in h_dev[side]:
                push(hs.at[r, side], hb.at[r, side, m], h_sem.at[r], dev)

    def edge_store(r, table, arows):
        hi, lo = split(table)
        edge = dot_nt(ends, jnp.concatenate([hi, lo], axis=0))
        edge = edge[:, 0:NC] + edge[:, NC : 2 * NC]
        zb[r, m] = jnp.concatenate(arows + [edge[0:1], edge[1:2], cf, cl], axis=0)

    def edge_send(r):
        fan(zb.at[r, m], z_sem.at[r], z_dev)

    def table_send(r, table, arows):
        table_store(r, table, arows)
        rows_send(r)
        edge_store(r, table, arows)
        edge_send(r)

    def scal_store(s, rows):
        rows = jnp.sum(jnp.concatenate(rows + [zero_row] * (8 - len(rows)), axis=0), axis=1, keepdims=True)
        ps[s, pl.ds(me, 1), :] = sum(jnp.where(lane == float(k), rows[k : k + 1], 0.0) for k in range(3))

    def scal_fan(s, devs):
        fan(ps.at[s, pl.ds(me, 1)], p_sem.at[s], devs)

    def scal_total(s):
        arrive(ps.at[s, pl.ds(0, E * Z - 1)], p_sem.at[s])
        total = jnp.sum(ps[s], axis=0, keepdims=True)
        return [total[:, k : k + 1] for k in range(3)]

    def columns(r, avec):
        va[0:4, :] = avec
        tiles = [va[pl.ds(2 * row_blk[k] + h, 1), :] for k in range(SLOTS) for h in range(2)]
        prev = zb[r, lax.rem(m + Z - 1, Z), 5:6, :]
        nxt = zb[r, lax.rem(m + 1, Z), 4:5, :]
        return jnp.concatenate(tiles + [prev, nxt, jnp.zeros((NC - 10, NC), F32)], axis=0).T

    def table_end(r, table, cols):
        cl_prev = zb[r, lax.rem(m + Z - 1, Z), 7:8, :]
        cf_next = zb[r, lax.rem(m + 1, Z), 6:7, :]
        table = table + jnp.where(ciota_f == cl_prev, cols[:, 8:9], 0.0)
        table = table + jnp.where(ciota_f == cf_next, cols[:, 9:10], 0.0)
        arrive(hb.at[r], h_sem.at[r])
        from_prev, from_next = (sum(hb[r, side, k] for k in range(Z)) for side in range(2))
        rl_prev, rf_next = hb[r, 0, 0, 1:2, :], hb[r, 1, 0, 1:2, :]
        table = table + jnp.where(riota_f == rl_prev, from_prev[0:1], 0.0)
        table = table + jnp.where(riota_f == rf_next, from_next[0:1], 0.0)
        if r == 0:
            skip_r = jnp.where(rl_prev == rf, 1.0, 0.0)
            skip_c = jnp.where(cl_prev == cf, 1.0, 0.0)
            mine = (riota_f >= rf + skip_r) & (riota_f <= rl) & (ciota_f >= cf + skip_c) & (ciota_f <= cl)
            own[...] = jnp.where(mine, 1.0, 0.0)
        return table

    def z_end(r):
        arrive(zb.at[r, pl.ds(0, Z - 1)], z_sem.at[r])
        return sum(zb[r, k, 0:4, :] for k in range(Z))

    def b_end(r):
        arrive(bb.at[r, pl.ds(0, E - 1)], b_sem.at[r])
        return sum(bb[r, k] for k in range(E))

    def select(gval):
        hi, lo = split(gval)
        ubuf[...] = dot(row_s[...], jnp.concatenate([hi, lo], axis=1)).astype(BF16)

    def expand(cols, bvec):
        vb[...] = bvec

        def tile(k):
            brow = jnp.concatenate([vb[pl.ds(2 * col_blk[k] + h, 1), :] for h in range(2)], axis=1)
            acol = jnp.concatenate([cols[:, 2 * k + h : 2 * k + h + 1] for h in range(2)], axis=0)
            return dot(ubuf[SIDE * k : SIDE * (k + 1), :], col_t[k]) + acol + brow

        return tile

    def fold(v):
        v = jnp.sum(v.reshape(SIDE // 8, 8, SIDE), axis=0)
        return v[:, 0:NC] + v[:, NC:SIDE]

    def lanes(v):
        return jnp.sum(v, axis=0, keepdims=True)

    def inner(u, v):
        total = lanes(u[0] * v[0]) * (1.0 / Z) + lanes(u[1] * v[1]) * (1.0 / E)
        return total + lanes(own[...] * u[2] * v[2])

    def scatter():
        rsb[xy] = tabs[:, pl.ds(xy * chunk, chunk), :]
        for (yy, xx), dev in zip(xy_at, xy_dev):
            push(tabs.at[:, pl.ds((yy * XN + xx) * chunk, chunk)], rsb.at[xy], rs_sem, dev)

    def rows_out(devs):
        for ee, mm in devs:
            src = image.at[pl.ds((ee * Z + mm) * own_rows, own_rows)]
            push(src, parts.at[pl.ds(me * own_rows, own_rows)], part_sem, (ee, mm))

    def rows_back():
        arrive(parts.at[pl.ds(0, NC - own_rows)], part_sem)
        gathered[pl.ds(me * own_rows, own_rows), :] = jnp.sum(
            parts[...].reshape(E * Z, own_rows, NC), axis=0
        ) if own_rows > 1 else jnp.sum(parts[...], axis=0, keepdims=True)
        fan(gathered.at[pl.ds(me * own_rows, own_rows)], gath_sem, all_dev)

    effects = None
    for newton in range(2):
        final = newton == 1
        r = 2 * newton
        if not final:

            def cells(k):
                mu[k] = keep(k, jnp.ones((SIDE, SIDE), F32))
                return keep(k, fbuf[k].astype(F32) - 1.0)

            fetches[4].wait()
        else:

            def cells(k):
                rate = keep(k, jnp.exp(both * x0[k] - shrink * xq[k]))
                mu[k] = rate
                return keep(k, fbuf[k].astype(F32)) - rate

        bpart = collect(cells)
        b_store(r, bpart)
        if not final:
            table, arows = table_sums()
            table_store(r, table, arows)
            edge_store(r, table, arows)
            pl.semaphore_wait(barrier, len(greet))
            rows_send(r)
            b_send(r)
            edge_send(r)
        else:
            b_send(r)
            table, arows = table_sums()
            table_send(r, table, arows)
        if final:
            tabs[0] = eg[...] * own[...]
            tabs[1] = table
            scatter()
        ra = z_end(r)
        if final:
            ra = ra - RIDGE * effects[0]
        cols = columns(r, ra)
        rg = table_end(r, table, cols)
        if final:
            rg = rg - RIDGE * eg[...]
        r0g[...] = rg
        select(rg)
        rb = b_end(r)
        if final:
            rb = rb - RIDGE * effects[1]
        res = (ra, rb, rg)
        tile = expand(cols, rb)
        quad = []

        def cells(k):
            v = tile(k)
            x0[k] = v
            w = mu[k] * v
            quad.append(fold(w * v))
            return w

        bpart = collect(cells)
        scal_store(r, [inner(res, res), lanes(sum(quad))])
        scal_fan(r, far_dev)
        b_store(r + 1, bpart)
        b_send(r + 1)
        table, arows = table_sums()
        table_store(r + 1, table, arows)
        rows_send(r + 1)
        if final:
            image[...] = table
            rows_out(far_dev)
        scal_fan(r, mid_dev)
        edge_store(r + 1, table, arows)
        edge_send(r + 1)
        scal_fan(r, near_dev)
        if final:
            arrive(rsb.at[pl.ds(0, XY - 1)], rs_sem)
            rxb[zc] = sum(rsb[k] for k in range(XY))
            fan(rxb.at[zc], rx_sem, zc_dev)
            parts[pl.ds(me * own_rows, own_rows), :] = image[pl.ds(me * own_rows, own_rows), :]
            rows_out(mid_dev + near_dev)
        qa = z_end(r + 1) + RIDGE * ra
        cols = columns(r + 1, qa)
        qgv = table_end(r + 1, table, cols) + RIDGE * r0g[...]
        qg[...] = qgv
        select(qgv)
        qb = b_end(r + 1) + RIDGE * rb
        tile = expand(cols, qb)
        for k in range(SLOTS):
            xq[k] = tile(k)
        rr, rhr, _ = scal_total(r)
        rhr = rhr + RIDGE * rr
        step = rr / rhr

        quad = []
        for k in range(SLOTS):
            v = x0[k] - step * xq[k]
            quad.append(fold(mu[k] * (v * v)))
        qvec = (qa, qb, qg[...])
        res1 = (ra - step * qa, rb - step * qb, r0g[...] - step * qg[...])
        scal_store(r + 1, [inner(res1, res1), lanes(sum(quad)), inner(res1, qvec)])
        scal_fan(r + 1, all_dev)
        if final:
            rows_back()
            arrive(rxb.at[pl.ds(0, 2 * Z - 1)], rx_sem)
            agb[xy] = sum(rxb[k] for k in range(2 * Z))
            fan(agb.at[xy], ag_sem, xy_dev)
        rr1, curve, cross = scal_total(r + 1)
        beta = rr1 / rr
        curve = curve + RIDGE * rr1 + 2.0 * beta * cross + beta * beta * rhr
        c1 = rr1 / curve
        c0 = step + c1 * beta
        both, shrink = c0 + c1, c1 * step
        da = c0 * ra + c1 * (ra - step * qa)
        db = c0 * rb + c1 * (rb - step * qb)
        if not final:
            effects = (da, db)
            eg[...] = c0 * r0g[...] + c1 * (r0g[...] - step * qg[...])
        else:
            a_out[...] = effects[0] + da
            b_out[...] = effects[1] + db
            arrive(agb.at[pl.ds(0, XY - 1)], ag_sem)
            arrive(gathered.at[pl.ds(0, NC - own_rows)], gath_sem)
            for k in range(XY):
                was = agb[k, 0]
                res0 = agb[k, 1] - RIDGE * was
                img = gathered[chunk * k : chunk * (k + 1), :] + RIDGE * res0
                g_out[chunk * k : chunk * (k + 1), :] = was + (c0 * res0 + c1 * (res0 - step * img))

def publish(a, b, g, a_out, b_out, g_out, sems):
    copies = [pltpu.make_async_copy(src, dst, sems.at[k]) for k, (src, dst) in enumerate(((g, g_out), (a, a_out), (b, b_out)))]
    for copy in copies:
        copy.start()
    for copy in copies:
        copy.wait()


def per_device(dims, flows, routing, tile_block, exp_country, imp_country):
    Y, XN, Z = dims
    XY = Y * XN
    chunk = NC // XY
    dma = pltpu.SemaphoreType.DMA
    vmem = functools.partial(pl.BlockSpec, memory_space=pltpu.VMEM)
    cells = SLOTS * SIDE
    pair = (NC, NC)
    sems = [dma((4, 2))] * 4 + [dma((2,))] * 5
    a, b, g = pl.pallas_call(
        functools.partial(kernel, dims),
        out_shape=(pltpu.VMEM((4, NC), F32), pltpu.VMEM((8, NC), F32), pltpu.VMEM(pair, F32)),
        in_specs=[pl.BlockSpec(memory_space=pl.ANY)] * 5,
        out_specs=(vmem(), vmem(), vmem()),
        scratch_shapes=[
            pltpu.SMEM((SLOTS,), jnp.int32),
            pltpu.SMEM((routing.size,), jnp.int32),
            pltpu.VMEM((4, NC), jnp.int32),
            pltpu.VMEM((8, NC), jnp.int32),
            pltpu.VMEM((SLOTS, SIDE, SIDE), BF16),
            pltpu.VMEM((NC, cells), BF16),
            pltpu.VMEM((cells, NC), BF16),
            pltpu.VMEM((SLOTS, 2 * NC, SIDE), BF16),
            pltpu.VMEM((cells, NC), BF16),
            pltpu.VMEM((SLOTS, SIDE, SIDE), F32),
            pltpu.VMEM((SLOTS, SIDE, SIDE), F32),
            pltpu.VMEM((SLOTS, SIDE, SIDE), F32),
            pltpu.VMEM((cells, 2 * NC), BF16),
            pltpu.VMEM((SLOTS, SIDE, 2 * SIDE), BF16),
            pltpu.VMEM((cells, 2 * NC), BF16),
            pltpu.VMEM((8, NC), F32),
            pltpu.VMEM((8, NC), F32),
            pltpu.VMEM(pair, F32),
            pltpu.VMEM(pair, F32),
            pltpu.VMEM(pair, F32),
            pltpu.VMEM(pair, F32),
            pltpu.VMEM((2,) + pair, F32),
            pltpu.VMEM(pair, F32),
            pltpu.VMEM(pair, F32),
            pltpu.VMEM(pair, F32),
            pltpu.VMEM((4, Z, 8, NC), F32),
            pltpu.VMEM((4, 2 * XY, 8, NC), F32),
            pltpu.VMEM((4, 2, 2, NC), F32),
            pltpu.VMEM((4, 2, Z, 2, NC), F32),
            pltpu.VMEM((4, 2 * XY * Z, NC), F32),
            pltpu.VMEM((XY, 2, chunk, NC), F32),
            pltpu.VMEM((2 * Z, 2, chunk, NC), F32),
            pltpu.VMEM((XY, 2, chunk, NC), F32),
            dma((5,)),
        ]
        + sems,
        compiler_params=pltpu.CompilerParams(collective_id=0, has_side_effects=True),
        name="gravity",
    )(
        routing.reshape(-1),
        tile_block,
        flows,
        exp_country.reshape(4, NC),
        imp_country.reshape(8, NC),
    )
    a, b, g = pl.pallas_call(
        publish,
        out_shape=(
            jax.ShapeDtypeStruct((4, NC), F32),
            jax.ShapeDtypeStruct((8, NC), F32),
            jax.ShapeDtypeStruct(pair, F32),
        ),
        in_specs=[pl.BlockSpec(memory_space=pl.ANY)] * 3,
        out_specs=(pl.BlockSpec(memory_space=pl.ANY),) * 3,
        scratch_shapes=[pltpu.SemaphoreType.DMA((3,))],
        name="publish",
    )(*(pltpu.with_memory_space_constraint(v, pltpu.VMEM) for v in (a, b, g)))
    return a.reshape(-1), b.reshape(-1), g


def solution(mesh, xn=4):
    dims = (mesh.shape["exp"] // (2 * xn), xn, mesh.shape["imp"])
    placed = (
        P(("exp", "imp"), None, None),
        P(("exp", "imp"), None, None),
        P(("exp", "imp")),
        P("exp"),
        P("imp"),
    )
    return jax.shard_map(
        functools.partial(per_device, dims),
        mesh=mesh,
        in_specs=placed,
        out_specs=(P("exp"), P("imp"), P()),
        check_vma=False,
    )
```
